256 devices in a mesh: net: 32 (over y, z), pat: 8 (over x, core).
Axes of the slice: x: 4, y: 4, z: 8, core: 2. Of those that a mesh axis runs over, the one named last changes fastest.
Arguments:
- tile_store: bfloat16 [1024, 128, 128], P('net'), may hold values from -0.1875 to 0.1875
- send_order: int32 [32, 32], P('net'), may hold values from 0 to 31, each once within a row
- place: int32 [32, 32], P('net'), may hold values from 0 to 31, each once within a row
- offsets: int32 [128, 8], P('net'), may hold values from 0 to 4
- state: int32 [16384, 8192], P('net', 'pat'), may hold values from 0 to 2
- drive: float32 [16384], P('net'), may hold values from 0.5 to 2
- conduct: float32 [16384], P('net'), may hold values from 1 to 4
- cotangent: bfloat16 [16384, 8192], P('net', 'pat'), may hold values from -6 to 6
Outputs:
- response: float32 [16384, 8192], P('net', 'pat')
- source_grad: float32 [16384, 8192], P('net', 'pat')
- tile_grad: float32 [8, 128, 128, 128], P('pat', 'net')
The draws below stay inside these ranges and needn't reach their ends.
All inputs are finite; a program needn't handle non-finite values.
Results may differ from the reference program's by a relative error of at most 0.004.
Values may be sent and summed in bfloat16 or wider, within the bound.
A program may use at most 128 MiB of HBM per device.

```python
import math
import jax
import jax.numpy as jnp

T_SIZE = 128
K = 8
ROWT = 4
HALO_T = 2
P_DEV = 1024
NROWT = 128
NROWS = 16384
PATTERNS = 8192
SLOTS = 1024
N_NET = 32
N_PAT = 8


def with_ends(result, key, least, high):
    shape = result.shape
    index_at = [jax.random.randint(jax.random.fold_in(key, axis), (), 0, shape[axis]) for axis in range(len(shape))]
    result = result.at[tuple(index_at)].set(least)
    longest = shape.index(max(shape))
    index_at[longest] = (index_at[longest] + 1) % shape[longest]
    return result.at[tuple(index_at)].set(high)


def level_of(key, extent, shards, low, top_value):
    def one(position, blocks):
        steps = jax.random.uniform(jax.random.fold_in(jax.random.fold_in(key, 6), position), (blocks,), jnp.float32, low / len(shards), top_value / len(shards))
        return jnp.repeat(jnp.exp(steps), extent[position] // blocks).reshape((-1,) + (1,) * (len(extent) - position - 1))

    gain = one(*shards[0])
    for cut in shards[1:]:
        gain = gain * one(*cut)
    return gain


def bell_draw(stream_key, shape, deviation, most, pieces=(), held_as=jnp.bfloat16):
    values = deviation * jax.random.normal(stream_key, shape, jnp.float32)
    if pieces:
        values = values * level_of(stream_key, shape, pieces, -0.22, 0.18)
    return jnp.clip(values, -most, most).astype(held_as)


def setup_inputs(seed: int = 0) -> dict:
    streams_of = jax.random.split(jax.random.key(seed), 9)
    tile_store = bell_draw(streams_of[0], (SLOTS, T_SIZE, T_SIZE), (K * T_SIZE) ** -0.5, 0.1875, ((0, 32),))
    send_order = jax.vmap(lambda own: jax.random.permutation(own, ROWT * K))(jax.random.split(streams_of[1], N_NET)).reshape((N_NET, ROWT * K)).astype(jnp.int32)
    place = jax.vmap(lambda own: jax.random.permutation(own, ROWT * K))(jax.random.split(streams_of[2], N_NET)).reshape((N_NET, ROWT * K)).astype(jnp.int32)
    offsets = with_ends(jax.random.randint(streams_of[3], (NROWT, K), 0, 2 * HALO_T + 1), jax.random.fold_in(streams_of[3], 1), 0, 2 * HALO_T).astype(jnp.int32)
    state = with_ends(jax.random.randint(streams_of[4], (NROWS, PATTERNS), 0, 3), jax.random.fold_in(streams_of[4], 1), 0, 2).astype(jnp.int32)
    drive = jnp.clip(jnp.exp(math.log(2.0) - 1.3862944 * jax.random.uniform(streams_of[5], (NROWS,), jnp.float32) ** level_of(streams_of[5], (NROWS,), ((0, 32),), -0.2, 0.2)), 0.5, 2.0)
    conduct = jnp.clip(jnp.exp(math.log(4.0) - 1.3862944 * jax.random.uniform(streams_of[6], (NROWS,), jnp.float32) ** level_of(streams_of[6], (NROWS,), ((0, 32),), -0.2, 0.2)), 1.0, 4.0)
    cotangent = bell_draw(streams_of[7], (NROWS, PATTERNS), 1.0, 6.0, ((0, 32), (1, 8)))
    return {"tile_store": tile_store, "send_order": send_order, "place": place, "offsets": offsets, "state": state, "drive": drive, "conduct": conduct, "cotangent": cotangent}


def reference(tile_store, send_order, place, offsets, state, drive, conduct, cotangent):
    width = ROWT * K
    share = width // N_NET
    owner = jnp.arange(N_NET, dtype=jnp.int32)[:, None]
    source_dev = place // share
    within = place % share
    outgoing = owner * share + within
    slot = source_dev * width + send_order[source_dev, outgoing]
    tiles = tile_store[slot].reshape(NROWT, K, T_SIZE, T_SIZE)
    tiles_f = tiles.astype(jnp.float32)
    gains = conduct[:, None]
    index = jnp.arange(NROWT, dtype=jnp.int32)[:, None] + offsets
    scale = 1.0 / jnp.sqrt(jnp.float32(PATTERNS))
    responses = []
    grads = []
    total = jnp.zeros((K, NROWT, T_SIZE, T_SIZE), jnp.float32)
    for group in range(N_PAT):
        levels = state[:, group * P_DEV:(group + 1) * P_DEV].astype(jnp.float32) - 1.0
        source = drive[:, None] * levels
        volt0 = (source / gains).astype(jnp.bfloat16)
        padded = jnp.pad(volt0.reshape(NROWT, T_SIZE, P_DEV), ((HALO_T, HALO_T), (0, 0), (0, 0)))
        columns = padded[index].astype(jnp.float32)
        coupled = jnp.einsum('ikab,ikbp->iap', tiles_f, columns).reshape(NROWS, P_DEV)
        responses.append((source - coupled) / gains)
        lam_full = cotangent[:, group * P_DEV:(group + 1) * P_DEV].astype(jnp.float32) / gains
        lam = lam_full.astype(jnp.bfloat16).astype(jnp.float32).reshape(NROWT, T_SIZE, P_DEV)
        terms = jnp.einsum('ikab,iap->ikbp', tiles_f, lam)
        back_pad = jnp.zeros((NROWT + 2 * HALO_T, T_SIZE, P_DEV), jnp.float32)
        for kk in range(K):
            back_pad = back_pad.at[index[:, kk]].add(terms[:, kk])
        back = back_pad[HALO_T:HALO_T + NROWT].reshape(NROWS, P_DEV)
        grads.append(lam_full - back / gains)
        total = total + jnp.einsum('iap,ikbp->kiab', lam, columns)
    response = jnp.concatenate(responses, axis=1)
    source_grad = jnp.concatenate(grads, axis=1)
    return (response, source_grad, -scale * total)
```

```python
import jax
import jax.numpy as jnp
from jax import lax
from jax.sharding import PartitionSpec as P

HALO_T = 2


def shifted(array, by):
    peers = lax.axis_size("net")
    pairs = [(i, i + by) for i in range(peers) if 0 <= i + by < peers]
    return lax.ppermute(array, "net", pairs)


def body(tile_store, send_order, place, offsets, state, drive, conduct, cotangent):
    tile = tile_store.shape[1]
    rows = drive.shape[0]
    row_tiles = rows // tile
    count_k = offsets.shape[1]
    patterns = cotangent.shape[1]
    groups = lax.axis_size("pat")
    width = HALO_T * tile
    wide = row_tiles + 2 * HALO_T
    gains = conduct[:, None]
    levels = state.astype(jnp.float32) - 1.0
    source = drive[:, None] * levels
    volt0 = (source / gains).astype(jnp.bfloat16)
    low = shifted(volt0[rows - width :], 1)
    high = shifted(volt0[:width], -1)
    outgoing = tile_store[send_order[0]]
    received = lax.all_to_all(outgoing, "net", split_axis=0, concat_axis=0, tiled=True)
    tiles = received[place[0]].reshape(row_tiles, count_k, tile, tile)
    index = jnp.arange(row_tiles, dtype=jnp.int32)[:, None] + offsets
    pick = (index[:, :, None] == jnp.arange(wide)[None, None, :]).astype(jnp.bfloat16)
    band = jnp.einsum("ikj,ikab->iajb", pick, tiles, preferred_element_type=jnp.float32)
    band = band.astype(jnp.bfloat16).reshape(rows, wide * tile)
    lam_full = cotangent.astype(jnp.float32) / gains
    lam = lam_full.astype(jnp.bfloat16)
    back_pad = lax.dot_general(
        band, lam, (((0,), (0,)), ((), ())), preferred_element_type=jnp.float32
    )
    from_upper = shifted(back_pad[:width].astype(jnp.bfloat16), -1)
    from_lower = shifted(back_pad[width + rows :].astype(jnp.bfloat16), 1)
    padded = jnp.concatenate([low, volt0, high], axis=0)
    scale = 1.0 / jnp.sqrt(jnp.float32(patterns * groups))
    outer = lax.dot_general(
        lam, padded, (((1,), (1,)), ((), ())), preferred_element_type=jnp.float32
    )
    outer = (-scale * outer).astype(jnp.bfloat16).reshape(row_tiles, tile, wide, tile)
    shares = jnp.einsum(
        "ikj,iajb->kiab", pick, outer, preferred_element_type=jnp.bfloat16
    )
    shares = lax.all_to_all(shares, "pat", split_axis=0, concat_axis=0, tiled=True)
    tile_grad = jnp.sum(shares.astype(jnp.float32), axis=0, keepdims=True)
    coupled = jnp.dot(band, padded, preferred_element_type=jnp.float32)
    response = (source - coupled) / gains
    back = back_pad[width : width + rows]
    extra = jnp.concatenate([from_lower, from_upper], axis=0).astype(jnp.float32)
    source_grad = lam_full - (back + extra) / gains
    return (response, source_grad, tile_grad)


def solution(mesh):
    placed = (
        P("net", None, None),
        P("net", None),
        P("net", None),
        P("net", None),
        P("net", "pat"),
        P("net"),
        P("net"),
        P("net", "pat"),
    )
    return jax.shard_map(
        body,
        mesh=mesh,
        in_specs=placed,
        out_specs=(P("net", "pat"), P("net", "pat"), P("pat", "net", None, None)),
        check_vma=False,
    )
```

```python
import jax
import jax.numpy as jnp
from jax import lax
from jax.experimental import pallas as pl
from jax.experimental.pallas import tpu as pltpu
from jax.sharding import PartitionSpec as P

MESH = pl.DeviceIdType.MESH
BF16 = jnp.bfloat16
F32 = jnp.float32
T = 128
ROWT = 4
K = 8
ROWS = 512
PATS = 1024
HALO = 256
NET = 32
NZ = 8
NY = 4
NX = 4
COLS = 256
CHUNKS = PATS // COLS


def mod(value, size):
    return lax.rem(value + 4 * size, size)


def dot(a, b, dims):
    return lax.dot_general(a, b, (dims, ((), ())), preferred_element_type=F32)


def kernel(
    scale,
    drive,
    conduct,
    order,
    place,
    offsets,
    store_hbm,
    state_hbm,
    cot_hbm,
    resp,
    sgrad,
    tgrad,
    store,
    stage,
    tiles,
    state,
    cot,
    vpad,
    lam,
    band,
    drive_b,
    recip_b,
    psend,
    precv,
    gsum,
    asend,
    arecv,
    bsend,
    brecv,
    load_sem,
    route_s,
    route_r,
    volt_s,
    volt_r,
    across_s,
    across_r,
    core_s,
    core_r,
    back_s,
    back_r,
    pair_s,
    pair_r,
    grad_s,
    grad_r,
):
    n = lax.axis_index("net")
    g = lax.axis_index("pat")
    y, z = n // NZ, lax.rem(n, NZ)
    x, c = g // 2, lax.rem(g, 2)
    mate = g + 1 - 2 * c

    def at_x(by, core):
        return mod(x + by, NX) * 2 + core

    def remote(src, dst, send, recv, net, pat):
        return pltpu.make_async_remote_copy(
            src_ref=src,
            dst_ref=dst,
            send_sem=send,
            recv_sem=recv,
            device_id=(net, pat),
            device_id_type=MESH,
        )

    barrier = pltpu.get_barrier_semaphore()

    def greet(net, pat):
        pl.semaphore_signal(barrier, inc=1, device_id=(net, pat), device_id_type=MESH)

    def source_net(m):
        return mod(y - m, NY) * NZ + mod(z - g - 2 * m, NZ)

    def target_net(m):
        return mod(y + m, NY) * NZ + mod(z + g + 2 * m, NZ)

    for m in (1, 2, 3):
        greet(source_net(m), g)

    @pl.when(g != 0)
    def _():
        greet(source_net(0), g)

    for by in (1, 2, 3):
        greet(n, at_x(by, c))
    greet(n, mate)

    @pl.when(n > 0)
    def _():
        greet(n - 1, g)

    @pl.when(n < NET - 1)
    def _():
        greet(n + 1, g)

    loads = []
    for r in (0, 3, 1, 2):
        rows = pl.ds(r * T, T)
        loads.append(
            pltpu.make_async_copy(state_hbm.at[rows], state.at[rows], load_sem.at[r])
        )
    store_load = pltpu.make_async_copy(store_hbm, store, load_sem.at[8])
    cot_loads = []
    for r in range(ROWT):
        rows = pl.ds(r * T, T)
        cot_loads.append(
            pltpu.make_async_copy(cot_hbm.at[rows], cot.at[rows], load_sem.at[4 + r])
        )
    store_load.start()
    for copy in loads + cot_loads:
        copy.start()

    eye = lax.broadcasted_iota(jnp.int32, (T, T), 0) == lax.broadcasted_iota(
        jnp.int32, (T, T), 1
    )
    ratio = []
    for r in range(ROWT):
        d_row = jnp.broadcast_to(drive[r : r + 1, :], (T, T))
        g_row = jnp.broadcast_to(conduct[r : r + 1, :], (T, T))
        d_col = jnp.sum(jnp.where(eye, d_row, 0.0), axis=1, keepdims=True)
        g_col = jnp.sum(jnp.where(eye, g_row, 0.0), axis=1, keepdims=True)
        drive_b[r * T : (r + 1) * T, :] = jnp.broadcast_to(d_col, (T, T))
        recip_b[r * T : (r + 1) * T, :] = jnp.broadcast_to(1.0 / g_col, (T, T))
        ratio.append((d_col / g_col).astype(BF16).astype(F32))

    store_load.wait()
    for m in range(ROWT):
        stage[m] = store[order[0, target_net(m)]]

    @pl.when(g == 0)
    def _():
        tiles[0] = store[order[0, n]]

    for copy, r in zip(loads, (0, 3, 1, 2)):
        copy.wait()
        rows = slice(r * T, (r + 1) * T)
        levels = state[rows, :].astype(F32) - 1.0
        vpad[HALO + r * T : HALO + (r + 1) * T, :] = (levels * ratio[r]).astype(BF16)

    @pl.when(n == 0)
    def _():
        vpad[0:HALO, :] = jnp.zeros((HALO, PATS), BF16)

    @pl.when(n == NET - 1)
    def _():
        vpad[HALO + ROWS :, :] = jnp.zeros((HALO, PATS), BF16)

    peers = (
        7
        + jnp.where(g != 0, 1, 0)
        + jnp.where(n > 0, 1, 0)
        + jnp.where(n < NET - 1, 1, 0)
    )
    pl.semaphore_wait(barrier, peers)

    route = [
        remote(
            stage.at[m],
            tiles.at[g * ROWT + m],
            route_s.at[m],
            route_r.at[m],
            target_net(m),
            g,
        )
        for m in range(ROWT)
    ]

    @pl.when(g != 0)
    def _():
        route[0].start()

    for m in (1, 2, 3):
        route[m].start()

    volt_down, volt_up = [], []
    for h in (0, 1):
        volt_down.append(
            remote(
                vpad.at[pl.ds(HALO + h * T, T)],
                vpad.at[pl.ds(HALO + ROWS + h * T, T)],
                volt_s.at[h],
                volt_r.at[h],
                n - 1,
                g,
            )
        )
        volt_up.append(
            remote(
                vpad.at[pl.ds(HALO + ROWS - HALO + h * T, T)],
                vpad.at[pl.ds(h * T, T)],
                volt_s.at[2 + h],
                volt_r.at[2 + h],
                n + 1,
                g,
            )
        )

    @pl.when(n > 0)
    def _():
        for copy in volt_down:
            copy.start()

    @pl.when(n < NET - 1)
    def _():
        for copy in volt_up:
            copy.start()

    for r in range(ROWT):
        cot_loads[r].wait()
        rows = slice(r * T, (r + 1) * T)
        lam[rows, :] = (
            cot[rows, :].astype(F32) * jnp.broadcast_to(recip_b[rows, :1], (T, PATS))
        ).astype(BF16)

    for i in range(ROWT):
        for j in range(K):
            if j < i or j > i + 4:
                band[i * T : (i + 1) * T, j * T : (j + 1) * T] = jnp.zeros((T, T), BF16)

    across, relay = [], []
    for m in range(ROWT):
        if m == 0:

            @pl.when(g != 0)
            def _():
                route[0].wait_recv()
        else:
            route[m].wait_recv()
        mine = tiles.at[g * ROWT + m]
        for by in (1, 3, 2):
            copy = remote(
                mine, mine, across_s.at[by - 1, m], across_r.at[by - 1, m], n, at_x(by, c)
            )
            copy.start()
            across.append(copy)
        copy = remote(mine, mine, core_s.at[0, m], core_r.at[0, m], n, mate)
        copy.start()
        relay.append(copy)
    for m in range(ROWT):
        for by in (1, 3, 2):
            slot = tiles.at[at_x(-by, c) * ROWT + m]
            remote(
                slot, slot, across_s.at[by - 1, m], across_r.at[by - 1, m], n, at_x(by, c)
            ).wait_recv()
            copy = remote(slot, slot, core_s.at[by, m], core_r.at[by, m], n, mate)
            copy.start()
            relay.append(copy)
    for m in range(ROWT):
        for by in (0, 1, 3, 2):
            slot = tiles.at[at_x(-by, 1 - c) * ROWT + m]
            remote(slot, slot, core_s.at[by, m], core_r.at[by, m], n, mate).wait_recv()

    def tile_of(i, k):
        owner = place[0, i * K + k]
        m = lax.rem(y - owner // NZ + NY, NY)
        lane = lax.rem(z - lax.rem(owner, NZ) - 2 * m + 4 * NZ, NZ)
        return tiles[lane * ROWT + m].astype(F32)

    def fill(i, d):
        total = jnp.zeros((T, T), F32)
        for k in range(K):
            total += tile_of(i, k) * (offsets[i, k] == d).astype(F32)
        band[i * T : (i + 1) * T, (i + d) * T : (i + d + 1) * T] = total.astype(BF16)

    first = ((0, 0), (0, 1), (1, 0), (2, 4), (3, 3), (3, 4))
    for i, d in first:
        fill(i, d)

    back_down, back_up = [], []
    for q in range(CHUNKS):
        cols = slice(q * COLS, (q + 1) * COLS)
        psend[0, q] = dot(band[0:HALO, 0:HALO], lam[0:HALO, cols], ((0,), (0,))).astype(BF16)
        psend[1, q] = dot(
            band[HALO:ROWS, 3 * HALO :], lam[HALO:ROWS, cols], ((0,), (0,))
        ).astype(BF16)
        back_down.append(
            remote(psend.at[0, q], precv.at[1, q], back_s.at[0, q], back_r.at[1, q], n - 1, g)
        )
        back_up.append(
            remote(psend.at[1, q], precv.at[0, q], back_s.at[1, q], back_r.at[0, q], n + 1, g)
        )

        @pl.when(n > 0)
        def _():
            back_down[q].start()

        @pl.when(n < NET - 1)
        def _():
            back_up[q].start()

    for i in range(ROWT):
        for d in range(5):
            if (i, d) not in first:
                fill(i, d)

    @pl.when(n > 0)
    def _():
        for copy in volt_up:
            copy.wait_recv()

    @pl.when(n < NET - 1)
    def _():
        for copy in volt_down:
            copy.wait_recv()

    for half in (0, 1):

        def outer(jb, carry):
            start = pl.multiple_of(half * HALO + jb * HALO, HALO)
            block = dot(
                lam[half * HALO : (half + 1) * HALO, :],
                vpad[pl.ds(start, HALO), :],
                ((1,), (1,)),
            )
            for ii in (0, 1):
                for jj in (0, 1):
                    gsum[(2 * half + ii) * 6 + 2 * jb + jj] = (
                        block[ii * T : (ii + 1) * T, jj * T : (jj + 1) * T] * -scale
                    )
            return carry

        lax.fori_loop(0, 3, outer, 0)

    def share(i, k):
        return gsum[i * 6 + i % 2 + offsets[i, k]]

    pair = []
    for by in (1, 2, 3, 0):
        for i in range(ROWT):
            asend[by, i] = share(i, at_x(by, 1 - c)).astype(BF16)
        copy = remote(asend.at[by], arecv.at[by], pair_s.at[by], pair_r.at[by], n, mate)
        copy.start()
        pair.append(copy)

    def forward(q, carry):
        cols = pl.ds(pl.multiple_of(q * COLS, COLS), COLS)
        for half in (0, 1):
            rows = slice(half * HALO, (half + 1) * HALO)
            coupled = dot(
                band[rows, half * HALO : half * HALO + 3 * HALO],
                vpad[half * HALO : half * HALO + 3 * HALO, cols],
                ((1,), (0,)),
            )
            for s in range(COLS // T):
                part = pl.ds(pl.multiple_of(q * COLS + s * T, T), T)
                source = drive_b[rows, :] * (state[rows, part].astype(F32) - 1.0)
                resp[rows, part] = (source - coupled[:, s * T : (s + 1) * T]) * recip_b[rows, :]
        return carry

    lax.fori_loop(0, CHUNKS, forward, 0)

    grad = []
    for by, copy in zip((1, 2, 3), pair):
        copy.wait_recv()
        for i in range(ROWT):
            bsend[by - 1, i] = (share(i, at_x(by, c)) + arecv[by, i].astype(F32)).astype(BF16)
        copy = remote(
            bsend.at[by - 1], brecv.at[by - 1], grad_s.at[by - 1], grad_r.at[by - 1], n, at_x(by, c)
        )
        copy.start()
        grad.append(copy)

    def backward(q, carry):
        cols = pl.ds(pl.multiple_of(q * COLS, COLS), COLS)
        for half in (0, 1):
            rows = slice(half * HALO, (half + 1) * HALO)
            back = dot(
                band[:, HALO + half * HALO : 2 * HALO + half * HALO],
                lam[:, cols],
                ((0,), (0,)),
            )
            for s in range(COLS // T):
                part = pl.ds(pl.multiple_of(q * COLS + s * T, T), T)
                sgrad[rows, part] = (
                    cot[rows, part].astype(F32) - back[:, s * T : (s + 1) * T]
                ) * recip_b[rows, :]
        return carry

    lax.fori_loop(0, CHUNKS, backward, 0)

    pair[3].wait_recv()
    for copy in grad:
        copy.wait_recv()
    for i in range(ROWT):
        total = share(i, g) + arecv[0, i].astype(F32)
        for by in (1, 2, 3):
            total += brecv[by - 1, i].astype(F32)
        tgrad[0, i] = total

    def add(side, q):
        rows = slice(side * HALO, (side + 1) * HALO)
        for s in range(COLS // T):
            part = slice(q * COLS + s * T, q * COLS + (s + 1) * T)
            terms = precv[side, q, :, s * T : (s + 1) * T].astype(F32)
            sgrad[rows, part] -= terms * recip_b[rows, :]

    for q in range(CHUNKS):

        @pl.when(n > 0)
        def _():
            back_up[q].wait_recv()
            add(0, q)

        @pl.when(n < NET - 1)
        def _():
            back_down[q].wait_recv()
            add(1, q)

    @pl.when(g != 0)
    def _():
        route[0].wait_send()

    for copy in route[1:] + across + relay + pair + grad:
        copy.wait_send()

    @pl.when(n > 0)
    def _():
        for copy in volt_down + back_down:
            copy.wait_send()

    @pl.when(n < NET - 1)
    def _():
        for copy in volt_up + back_up:
            copy.wait_send()


def body(tile_store, send_order, place, offsets, state, drive, conduct, cotangent):
    groups = lax.axis_size("pat")
    scale = 1.0 / float(PATS * groups) ** 0.5
    smem = pl.BlockSpec(memory_space=pltpu.SMEM)
    vmem = pl.BlockSpec(memory_space=pltpu.VMEM)
    hbm = pl.BlockSpec(memory_space=pltpu.HBM)
    dma = pltpu.SemaphoreType.DMA

    def run(*refs):
        kernel(scale, *refs)

    return pl.pallas_call(
        run,
        out_shape=(
            jax.ShapeDtypeStruct((ROWS, PATS), F32),
            jax.ShapeDtypeStruct((ROWS, PATS), F32),
            jax.ShapeDtypeStruct((1, ROWT, T, T), F32),
        ),
        in_specs=[vmem, vmem, smem, smem, smem, hbm, hbm, hbm],
        out_specs=(vmem, vmem, vmem),
        scratch_shapes=[
            pltpu.VMEM((NET, T, T), BF16),
            pltpu.VMEM((ROWT, T, T), BF16),
            pltpu.VMEM((NET, T, T), BF16),
            pltpu.VMEM((ROWS, PATS), jnp.int32),
            pltpu.VMEM((ROWS, PATS), BF16),
            pltpu.VMEM((ROWS + 2 * HALO, PATS), BF16),
            pltpu.VMEM((ROWS, PATS), BF16),
            pltpu.VMEM((ROWS, ROWS + 2 * HALO), BF16),
            pltpu.VMEM((ROWS, T), F32),
            pltpu.VMEM((ROWS, T), F32),
            pltpu.VMEM((2, CHUNKS, HALO, COLS), BF16),
            pltpu.VMEM((2, CHUNKS, HALO, COLS), BF16),
            pltpu.VMEM((24, T, T), F32),
            pltpu.VMEM((NX, ROWT, T, T), BF16),
            pltpu.VMEM((NX, ROWT, T, T), BF16),
            pltpu.VMEM((NX - 1, ROWT, T, T), BF16),
            pltpu.VMEM((NX - 1, ROWT, T, T), BF16),
            dma((9,)),
            dma((ROWT,)),
            dma((ROWT,)),
            dma((4,)),
            dma((4,)),
            dma((3, ROWT)),
            dma((3, ROWT)),
            dma((4, ROWT)),
            dma((4, ROWT)),
            dma((2, CHUNKS)),
            dma((2, CHUNKS)),
            dma((NX,)),
            dma((NX,)),
            dma((NX - 1,)),
            dma((NX - 1,)),
        ],
        compiler_params=pltpu.CompilerParams(
            collective_id=0, has_side_effects=True, vmem_limit_bytes=40 * 1024 * 1024
        ),
        name="crosstalk",
    )(
        drive.reshape(ROWT, T),
        conduct.reshape(ROWT, T),
        send_order,
        place,
        offsets,
        tile_store,
        state,
        cotangent,
    )


def solution(mesh):
    placed = (
        P("net", None, None),
        P("net", None),
        P("net", None),
        P("net", None),
        P("net", "pat"),
        P("net"),
        P("net"),
        P("net", "pat"),
    )
    return jax.shard_map(
        body,
        mesh=mesh,
        in_specs=placed,
        out_specs=(P("net", "pat"), P("net", "pat"), P("pat", "net", None, None)),
        check_vma=False,
    )
```

```python
import jax
import jax.numpy as jnp
from jax import lax
from jax.experimental import pallas as pl
from jax.experimental.pallas import tpu as pltpu
from jax.sharding import PartitionSpec as P

MESH = pl.DeviceIdType.MESH
BF16 = jnp.bfloat16
F32 = jnp.float32
T = 128
ROWT = 4
K = 8
ROWS = 512
PATS = 1024
HALO = 256
NET = 32
NZ = 8
NY = 4
NX = 4
COLS = 256
CHUNKS = PATS // COLS


def mod(value, size):
    return lax.rem(value + 4 * size, size)


def dot(a, b, dims):
    return lax.dot_general(a, b, (dims, ((), ())), preferred_element_type=F32)


def kernel(
    scale,
    drive_hbm,
    conduct_hbm,
    order_hbm,
    place_hbm,
    offsets_hbm,
    store_hbm,
    state_hbm,
    cot_hbm,
    resp,
    sgrad,
    tgrad,
    drive,
    conduct,
    order,
    place,
    offsets,
    store,
    stage,
    tiles,
    state,
    cot,
    vpad,
    lam,
    band,
    drive_b,
    recip_b,
    psend,
    precv,
    gsum,
    asend,
    arecv,
    bsend,
    brecv,
    load_sem,
    route_s,
    route_r,
    volt_s,
    volt_r,
    across_s,
    across_r,
    core_s,
    core_r,
    back_s,
    back_r,
    pair_s,
    pair_r,
    grad_s,
    grad_r,
):
    n = lax.axis_index("net")
    g = lax.axis_index("pat")
    y, z = n // NZ, lax.rem(n, NZ)
    x, c = g // 2, lax.rem(g, 2)
    mate = g + 1 - 2 * c

    def at_x(by, core):
        return mod(x + by, NX) * 2 + core

    def remote(src, dst, send, recv, net, pat):
        return pltpu.make_async_remote_copy(
            src_ref=src,
            dst_ref=dst,
            send_sem=send,
            recv_sem=recv,
            device_id=(net, pat),
            device_id_type=MESH,
        )

    barrier = pltpu.get_barrier_semaphore()

    def greet(net, pat):
        pl.semaphore_signal(barrier, inc=1, device_id=(net, pat), device_id_type=MESH)

    def source_net(m):
        return mod(y - m, NY) * NZ + mod(z - g - 2 * m, NZ)

    def target_net(m):
        return mod(y + m, NY) * NZ + mod(z + g + 2 * m, NZ)

    for m in (1, 2, 3):
        greet(source_net(m), g)

    @pl.when(g != 0)
    def _():
        greet(source_net(0), g)

    for by in (1, 2, 3):
        greet(n, at_x(by, c))
    greet(n, mate)

    @pl.when(n > 0)
    def _():
        greet(n - 1, g)

    @pl.when(n < NET - 1)
    def _():
        greet(n + 1, g)

    loads = []
    for r in (0, 3, 1, 2):
        rows = pl.ds(r * T, T)
        loads.append(
            pltpu.make_async_copy(state_hbm.at[rows], state.at[rows], load_sem.at[r])
        )
    store_load = pltpu.make_async_copy(store_hbm, store, load_sem.at[8])
    cot_loads = []
    for r in range(ROWT):
        rows = pl.ds(r * T, T)
        cot_loads.append(
            pltpu.make_async_copy(cot_hbm.at[rows], cot.at[rows], load_sem.at[4 + r])
        )
    small = [
        pltpu.make_async_copy(drive_hbm, drive, load_sem.at[9]),
        pltpu.make_async_copy(conduct_hbm, conduct, load_sem.at[10]),
        pltpu.make_async_copy(order_hbm, order, load_sem.at[11]),
        pltpu.make_async_copy(place_hbm, place, load_sem.at[12]),
        pltpu.make_async_copy(offsets_hbm, offsets, load_sem.at[13]),
    ]
    for copy in small + [store_load] + loads + cot_loads:
        copy.start()
    for copy in small:
        copy.wait()

    eye = lax.broadcasted_iota(jnp.int32, (T, T), 0) == lax.broadcasted_iota(
        jnp.int32, (T, T), 1
    )
    ratio = []
    for r in range(ROWT):
        d_row = jnp.broadcast_to(drive[r : r + 1, :], (T, T))
        g_row = jnp.broadcast_to(conduct[r : r + 1, :], (T, T))
        d_col = jnp.sum(jnp.where(eye, d_row, 0.0), axis=1, keepdims=True)
        g_col = jnp.sum(jnp.where(eye, g_row, 0.0), axis=1, keepdims=True)
        drive_b[r * T : (r + 1) * T, :] = jnp.broadcast_to(d_col, (T, T))
        recip_b[r * T : (r + 1) * T, :] = jnp.broadcast_to(1.0 / g_col, (T, T))
        ratio.append((d_col / g_col).astype(BF16).astype(F32))

    store_load.wait()
    for m in range(ROWT):
        stage[m] = store[order[0, target_net(m)]]

    @pl.when(g == 0)
    def _():
        tiles[0] = store[order[0, n]]

    for copy, r in zip(loads, (0, 3, 1, 2)):
        copy.wait()
        rows = slice(r * T, (r + 1) * T)
        levels = state[rows, :].astype(F32) - 1.0
        vpad[HALO + r * T : HALO + (r + 1) * T, :] = (levels * ratio[r]).astype(BF16)

    @pl.when(n == 0)
    def _():
        vpad[0:HALO, :] = jnp.zeros((HALO, PATS), BF16)

    @pl.when(n == NET - 1)
    def _():
        vpad[HALO + ROWS :, :] = jnp.zeros((HALO, PATS), BF16)

    peers = (
        7
        + jnp.where(g != 0, 1, 0)
        + jnp.where(n > 0, 1, 0)
        + jnp.where(n < NET - 1, 1, 0)
    )
    pl.semaphore_wait(barrier, peers)

    route = [
        remote(
            stage.at[m],
            tiles.at[g * ROWT + m],
            route_s.at[m],
            route_r.at[m],
            target_net(m),
            g,
        )
        for m in range(ROWT)
    ]

    @pl.when(g != 0)
    def _():
        route[0].start()

    for m in (1, 2, 3):
        route[m].start()

    volt_down, volt_up = [], []
    for h in (0, 1):
        volt_down.append(
            remote(
                vpad.at[pl.ds(HALO + h * T, T)],
                vpad.at[pl.ds(HALO + ROWS + h * T, T)],
                volt_s.at[h],
                volt_r.at[h],
                n - 1,
                g,
            )
        )
        volt_up.append(
            remote(
                vpad.at[pl.ds(HALO + ROWS - HALO + h * T, T)],
                vpad.at[pl.ds(h * T, T)],
                volt_s.at[2 + h],
                volt_r.at[2 + h],
                n + 1,
                g,
            )
        )

    @pl.when(n > 0)
    def _():
        for copy in volt_down:
            copy.start()

    @pl.when(n < NET - 1)
    def _():
        for copy in volt_up:
            copy.start()

    for r in range(ROWT):
        cot_loads[r].wait()
        rows = slice(r * T, (r + 1) * T)
        lam[rows, :] = (
            cot[rows, :].astype(F32) * jnp.broadcast_to(recip_b[rows, :1], (T, PATS))
        ).astype(BF16)

    for i in range(ROWT):
        for j in range(K):
            if j < i or j > i + 4:
                band[i * T : (i + 1) * T, j * T : (j + 1) * T] = jnp.zeros((T, T), BF16)

    across, relay = [], []
    for m in range(ROWT):
        if m == 0:

            @pl.when(g != 0)
            def _():
                route[0].wait_recv()
        else:
            route[m].wait_recv()
        mine = tiles.at[g * ROWT + m]
        for by in (1, 3, 2):
            copy = remote(
                mine, mine, across_s.at[by - 1, m], across_r.at[by - 1, m], n, at_x(by, c)
            )
            copy.start()
            across.append(copy)
        copy = remote(mine, mine, core_s.at[0, m], core_r.at[0, m], n, mate)
        copy.start()
        relay.append(copy)
    for m in range(ROWT):
        for by in (1, 3, 2):
            slot = tiles.at[at_x(-by, c) * ROWT + m]
            remote(
                slot, slot, across_s.at[by - 1, m], across_r.at[by - 1, m], n, at_x(by, c)
            ).wait_recv()
            copy = remote(slot, slot, core_s.at[by, m], core_r.at[by, m], n, mate)
            copy.start()
            relay.append(copy)
    for m in range(ROWT):
        for by in (0, 1, 3, 2):
            slot = tiles.at[at_x(-by, 1 - c) * ROWT + m]
            remote(slot, slot, core_s.at[by, m], core_r.at[by, m], n, mate).wait_recv()

    def tile_of(i, k):
        owner = place[0, i * K + k]
        m = lax.rem(y - owner // NZ + NY, NY)
        lane = lax.rem(z - lax.rem(owner, NZ) - 2 * m + 4 * NZ, NZ)
        return tiles[lane * ROWT + m].astype(F32)

    def fill(i, d):
        total = jnp.zeros((T, T), F32)
        for k in range(K):
            total += tile_of(i, k) * (offsets[i, k] == d).astype(F32)
        band[i * T : (i + 1) * T, (i + d) * T : (i + d + 1) * T] = total.astype(BF16)

    first = ((0, 0), (0, 1), (1, 0), (2, 4), (3, 3), (3, 4))
    for i, d in first:
        fill(i, d)

    back_down, back_up = [], []
    for q in range(CHUNKS):
        cols = slice(q * COLS, (q + 1) * COLS)
        psend[0, q] = dot(band[0:HALO, 0:HALO], lam[0:HALO, cols], ((0,), (0,))).astype(BF16)
        psend[1, q] = dot(
            band[HALO:ROWS, 3 * HALO :], lam[HALO:ROWS, cols], ((0,), (0,))
        ).astype(BF16)
        back_down.append(
            remote(psend.at[0, q], precv.at[1, q], back_s.at[0, q], back_r.at[1, q], n - 1, g)
        )
        back_up.append(
            remote(psend.at[1, q], precv.at[0, q], back_s.at[1, q], back_r.at[0, q], n + 1, g)
        )

        @pl.when(n > 0)
        def _():
            back_down[q].start()

        @pl.when(n < NET - 1)
        def _():
            back_up[q].start()

    for i in range(ROWT):
        for d in range(5):
            if (i, d) not in first:
                fill(i, d)

    @pl.when(n > 0)
    def _():
        for copy in volt_up:
            copy.wait_recv()

    @pl.when(n < NET - 1)
    def _():
        for copy in volt_down:
            copy.wait_recv()

    for half in (0, 1):

        def outer(jb, carry):
            start = pl.multiple_of(half * HALO + jb * HALO, HALO)
            block = dot(
                lam[half * HALO : (half + 1) * HALO, :],
                vpad[pl.ds(start, HALO), :],
                ((1,), (1,)),
            )
            for ii in (0, 1):
                for jj in (0, 1):
                    gsum[(2 * half + ii) * 6 + 2 * jb + jj] = (
                        block[ii * T : (ii + 1) * T, jj * T : (jj + 1) * T] * -scale
                    )
            return carry

        lax.fori_loop(0, 3, outer, 0)

    def share(i, k):
        return gsum[i * 6 + i % 2 + offsets[i, k]]

    pair = []
    for by in (1, 2, 3, 0):
        for i in range(ROWT):
            asend[by, i] = share(i, at_x(by, 1 - c)).astype(BF16)
        copy = remote(asend.at[by], arecv.at[by], pair_s.at[by], pair_r.at[by], n, mate)
        copy.start()
        pair.append(copy)

    def forward(q, carry):
        cols = pl.ds(pl.multiple_of(q * COLS, COLS), COLS)
        for half in (0, 1):
            rows = slice(half * HALO, (half + 1) * HALO)
            coupled = dot(
                band[rows, half * HALO : half * HALO + 3 * HALO],
                vpad[half * HALO : half * HALO + 3 * HALO, cols],
                ((1,), (0,)),
            )
            for s in range(COLS // T):
                part = pl.ds(pl.multiple_of(q * COLS + s * T, T), T)
                source = drive_b[rows, :] * (state[rows, part].astype(F32) - 1.0)
                resp[rows, part] = (source - coupled[:, s * T : (s + 1) * T]) * recip_b[rows, :]
        return carry

    lax.fori_loop(0, CHUNKS, forward, 0)

    grad = []
    for by, copy in zip((1, 2, 3), pair):
        copy.wait_recv()
        for i in range(ROWT):
            bsend[by - 1, i] = (share(i, at_x(by, c)) + arecv[by, i].astype(F32)).astype(BF16)
        copy = remote(
            bsend.at[by - 1], brecv.at[by - 1], grad_s.at[by - 1], grad_r.at[by - 1], n, at_x(by, c)
        )
        copy.start()
        grad.append(copy)

    def backward(q, carry):
        cols = pl.ds(pl.multiple_of(q * COLS, COLS), COLS)
        for half in (0, 1):
            rows = slice(half * HALO, (half + 1) * HALO)
            back = dot(
                band[:, HALO + half * HALO : 2 * HALO + half * HALO],
                lam[:, cols],
                ((0,), (0,)),
            )
            for s in range(COLS // T):
                part = pl.ds(pl.multiple_of(q * COLS + s * T, T), T)
                sgrad[rows, part] = (
                    cot[rows, part].astype(F32) - back[:, s * T : (s + 1) * T]
                ) * recip_b[rows, :]
        return carry

    lax.fori_loop(0, CHUNKS, backward, 0)

    pair[3].wait_recv()
    for copy in grad:
        copy.wait_recv()
    for i in range(ROWT):
        total = share(i, g) + arecv[0, i].astype(F32)
        for by in (1, 2, 3):
            total += brecv[by - 1, i].astype(F32)
        tgrad[0, i] = total

    def add(side, q):
        rows = slice(side * HALO, (side + 1) * HALO)
        for s in range(COLS // T):
            part = slice(q * COLS + s * T, q * COLS + (s + 1) * T)
            terms = precv[side, q, :, s * T : (s + 1) * T].astype(F32)
            sgrad[rows, part] -= terms * recip_b[rows, :]

    for q in range(CHUNKS):

        @pl.when(n > 0)
        def _():
            back_up[q].wait_recv()
            add(0, q)

        @pl.when(n < NET - 1)
        def _():
            back_down[q].wait_recv()
            add(1, q)

    @pl.when(g != 0)
    def _():
        route[0].wait_send()

    for copy in route[1:] + across + relay + pair + grad:
        copy.wait_send()

    @pl.when(n > 0)
    def _():
        for copy in volt_down + back_down:
            copy.wait_send()

    @pl.when(n < NET - 1)
    def _():
        for copy in volt_up + back_up:
            copy.wait_send()


def write_out(resp, sgrad, tgrad, resp_hbm, sgrad_hbm, tgrad_hbm, sem):
    copies = [
        pltpu.make_async_copy(src, dst, sem.at[i])
        for i, (src, dst) in enumerate(
            ((resp, resp_hbm), (sgrad, sgrad_hbm), (tgrad, tgrad_hbm))
        )
    ]
    for copy in copies:
        copy.start()
    for copy in copies:
        copy.wait()


def body(tile_store, send_order, place, offsets, state, drive, conduct, cotangent):
    groups = lax.axis_size("pat")
    scale = 1.0 / float(PATS * groups) ** 0.5
    vmem = pl.BlockSpec(memory_space=pltpu.VMEM)
    hbm = pl.BlockSpec(memory_space=pltpu.HBM)
    dma = pltpu.SemaphoreType.DMA

    def run(*refs):
        kernel(scale, *refs)

    held = pl.pallas_call(
        run,
        out_shape=(
            jax.ShapeDtypeStruct((ROWS, PATS), F32),
            jax.ShapeDtypeStruct((ROWS, PATS), F32),
            jax.ShapeDtypeStruct((1, ROWT, T, T), F32),
        ),
        in_specs=[hbm] * 8,
        out_specs=(vmem, vmem, vmem),
        scratch_shapes=[
            pltpu.VMEM((ROWT, T), F32),
            pltpu.VMEM((ROWT, T), F32),
            pltpu.SMEM((1, NET), jnp.int32),
            pltpu.SMEM((1, NET), jnp.int32),
            pltpu.SMEM((ROWT, K), jnp.int32),
            pltpu.VMEM((NET, T, T), BF16),
            pltpu.VMEM((ROWT, T, T), BF16),
            pltpu.VMEM((NET, T, T), BF16),
            pltpu.VMEM((ROWS, PATS), jnp.int32),
            pltpu.VMEM((ROWS, PATS), BF16),
            pltpu.VMEM((ROWS + 2 * HALO, PATS), BF16),
            pltpu.VMEM((ROWS, PATS), BF16),
            pltpu.VMEM((ROWS, ROWS + 2 * HALO), BF16),
            pltpu.VMEM((ROWS, T), F32),
            pltpu.VMEM((ROWS, T), F32),
            pltpu.VMEM((2, CHUNKS, HALO, COLS), BF16),
            pltpu.VMEM((2, CHUNKS, HALO, COLS), BF16),
            pltpu.VMEM((24, T, T), F32),
            pltpu.VMEM((NX, ROWT, T, T), BF16),
            pltpu.VMEM((NX, ROWT, T, T), BF16),
            pltpu.VMEM((NX - 1, ROWT, T, T), BF16),
            pltpu.VMEM((NX - 1, ROWT, T, T), BF16),
            dma((14,)),
            dma((ROWT,)),
            dma((ROWT,)),
            dma((4,)),
            dma((4,)),
            dma((3, ROWT)),
            dma((3, ROWT)),
            dma((4, ROWT)),
            dma((4, ROWT)),
            dma((2, CHUNKS)),
            dma((2, CHUNKS)),
            dma((NX,)),
            dma((NX,)),
            dma((NX - 1,)),
            dma((NX - 1,)),
        ],
        compiler_params=pltpu.CompilerParams(
            collective_id=0, has_side_effects=True, vmem_limit_bytes=40 * 1024 * 1024
        ),
        name="crosstalk",
    )(
        *[
            pltpu.with_memory_space_constraint(value, pltpu.HBM)
            for value in (
                drive.reshape(ROWT, T),
                conduct.reshape(ROWT, T),
                send_order,
                place,
                offsets,
                tile_store,
                state,
                cotangent,
            )
        ],
    )

    return pl.pallas_call(
        write_out,
        out_shape=[jax.ShapeDtypeStruct(value.shape, value.dtype) for value in held],
        in_specs=[vmem] * 3,
        out_specs=[hbm] * 3,
        scratch_shapes=[dma((3,))],
        compiler_params=pltpu.CompilerParams(vmem_limit_bytes=1024 * 1024),
        name="write_out",
    )(*held)


def solution(mesh):
    placed = (
        P("net", None, None),
        P("net", None),
        P("net", None),
        P("net", None),
        P("net", "pat"),
        P("net"),
        P("net"),
        P("net", "pat"),
    )
    return jax.shard_map(
        body,
        mesh=mesh,
        in_specs=placed,
        out_specs=(P("net", "pat"), P("net", "pat"), P("pat", "net", None, None)),
        check_vma=False,
    )
```

```python
import jax
import jax.numpy as jnp
from jax import lax
from jax.experimental import pallas as pl
from jax.experimental.pallas import tpu as pltpu
from jax.sharding import PartitionSpec as P

MESH = pl.DeviceIdType.MESH
BF16 = jnp.bfloat16
F32 = jnp.float32
T = 128
ROWT = 4
K = 8
ROWS = 512
PATS = 1024
HALO = 256
NET = 32
NZ = 8
NY = 4
NX = 4
COLS = 256
CHUNKS = PATS // COLS


def mod(value, size):
    return lax.rem(value + 4 * size, size)


def dot(a, b, dims):
    return lax.dot_general(a, b, (dims, ((), ())), preferred_element_type=F32)


def kernel(
    scale,
    drive_hbm,
    conduct_hbm,
    order_hbm,
    place_hbm,
    offsets_hbm,
    store_hbm,
    state_hbm,
    cot_hbm,
    resp,
    sgrad,
    tgrad,
    drive,
    conduct,
    order,
    place,
    offsets,
    store,
    stage,
    tiles,
    state,
    cot,
    vpad,
    lam,
    band,
    drive_b,
    recip_b,
    psend,
    precv,
    gsum,
    asend,
    arecv,
    hsend,
    hrecv,
    bsend,
    brecv,
    load_sem,
    route_s,
    route_r,
    volt_s,
    volt_r,
    across_s,
    across_r,
    core_s,
    core_r,
    back_s,
    back_r,
    pair_s,
    pair_r,
    hop_s,
    hop_r,
    grad_s,
    grad_r,
):
    n = lax.axis_index("net")
    g = lax.axis_index("pat")
    y, z = n // NZ, lax.rem(n, NZ)
    x, c = g // 2, lax.rem(g, 2)
    mate = g + 1 - 2 * c

    def at_x(by, core):
        return mod(x + by, NX) * 2 + core

    def remote(src, dst, send, recv, net, pat):
        return pltpu.make_async_remote_copy(
            src_ref=src,
            dst_ref=dst,
            send_sem=send,
            recv_sem=recv,
            device_id=(net, pat),
            device_id_type=MESH,
        )

    barrier = pltpu.get_barrier_semaphore()

    def greet(net, pat):
        pl.semaphore_signal(barrier, inc=1, device_id=(net, pat), device_id_type=MESH)

    def source_net(m):
        return mod(y - m, NY) * NZ + mod(z - g - 2 * m, NZ)

    def target_net(m):
        return mod(y + m, NY) * NZ + mod(z + g + 2 * m, NZ)

    for m in (1, 2, 3):
        greet(source_net(m), g)

    @pl.when(g != 0)
    def _():
        greet(source_net(0), g)

    for by in (1, 3):
        greet(n, at_x(by, c))
    greet(n, mate)

    @pl.when(n > 0)
    def _():
        greet(n - 1, g)

    @pl.when(n < NET - 1)
    def _():
        greet(n + 1, g)

    loads = []
    for r in (0, 3, 1, 2):
        rows = pl.ds(r * T, T)
        loads.append(
            pltpu.make_async_copy(state_hbm.at[rows], state.at[rows], load_sem.at[r])
        )
    store_load = pltpu.make_async_copy(store_hbm, store, load_sem.at[8])
    cot_loads = []
    for r in range(ROWT):
        rows = pl.ds(r * T, T)
        cot_loads.append(
            pltpu.make_async_copy(cot_hbm.at[rows], cot.at[rows], load_sem.at[4 + r])
        )
    small = [
        pltpu.make_async_copy(drive_hbm, drive, load_sem.at[9]),
        pltpu.make_async_copy(conduct_hbm, conduct, load_sem.at[10]),
        pltpu.make_async_copy(order_hbm, order, load_sem.at[11]),
        pltpu.make_async_copy(place_hbm, place, load_sem.at[12]),
        pltpu.make_async_copy(offsets_hbm, offsets, load_sem.at[13]),
    ]
    for copy in small + [store_load] + loads + cot_loads:
        copy.start()
    for copy in small:
        copy.wait()

    eye = lax.broadcasted_iota(jnp.int32, (T, T), 0) == lax.broadcasted_iota(
        jnp.int32, (T, T), 1
    )
    ratio = []
    for r in range(ROWT):
        d_row = jnp.broadcast_to(drive[r : r + 1, :], (T, T))
        g_row = jnp.broadcast_to(conduct[r : r + 1, :], (T, T))
        d_col = jnp.sum(jnp.where(eye, d_row, 0.0), axis=1, keepdims=True)
        g_col = jnp.sum(jnp.where(eye, g_row, 0.0), axis=1, keepdims=True)
        drive_b[r * T : (r + 1) * T, :] = jnp.broadcast_to(d_col, (T, T))
        recip_b[r * T : (r + 1) * T, :] = jnp.broadcast_to(1.0 / g_col, (T, T))
        ratio.append((d_col / g_col).astype(BF16).astype(F32))

    sent = []

    def only(condition, act):
        if condition is None:
            act()
        else:
            pl.when(condition)(act)

    def send(condition, copy):
        only(condition, copy.start)
        sent.append((condition, copy))

    has_low, has_high = n > 0, n < NET - 1

    def stage_tiles():
        store_load.wait()
        for m in range(ROWT):
            stage[m] = store[order[0, target_net(m)]]

        @pl.when(g == 0)
        def _():
            tiles[0] = store[order[0, n]]

    def make_volt():
        for copy, r in zip(loads, (0, 3, 1, 2)):
            copy.wait()
            rows = slice(r * T, (r + 1) * T)
            levels = state[rows, :].astype(F32) - 1.0
            vpad[HALO + r * T : HALO + (r + 1) * T, :] = (levels * ratio[r]).astype(BF16)

        @pl.when(n == 0)
        def _():
            vpad[0:HALO, :] = jnp.zeros((HALO, PATS), BF16)

        @pl.when(n == NET - 1)
        def _():
            vpad[HALO + ROWS :, :] = jnp.zeros((HALO, PATS), BF16)

    def enter():
        peers = (
            6
            + jnp.where(g != 0, 1, 0)
            + jnp.where(n > 0, 1, 0)
            + jnp.where(n < NET - 1, 1, 0)
        )
        pl.semaphore_wait(barrier, peers)

    route = [
        remote(
            stage.at[m],
            tiles.at[g * ROWT + m],
            route_s.at[m],
            route_r.at[m],
            target_net(m),
            g,
        )
        for m in range(ROWT)
    ]
    route_if = [g != 0, None, None, None]

    def send_tiles():
        for m in range(ROWT):
            send(route_if[m], route[m])

    volt_down, volt_up = [], []
    for h in (0, 1):
        volt_down.append(
            remote(
                vpad.at[pl.ds(HALO + h * T, T)],
                vpad.at[pl.ds(HALO + ROWS + h * T, T)],
                volt_s.at[h],
                volt_r.at[h],
                n - 1,
                g,
            )
        )
        volt_up.append(
            remote(
                vpad.at[pl.ds(ROWS + h * T, T)],
                vpad.at[pl.ds(h * T, T)],
                volt_s.at[2 + h],
                volt_r.at[2 + h],
                n + 1,
                g,
            )
        )

    def send_volt():
        for h in (0, 1):
            send(has_low, volt_down[h])
            send(has_high, volt_up[h])

    def wait_volt():
        for h in (0, 1):
            only(has_low, volt_up[h].wait_recv)
            only(has_high, volt_down[h].wait_recv)

    def make_lam():
        for r in range(ROWT):
            cot_loads[r].wait()
            rows = slice(r * T, (r + 1) * T)
            recip = jnp.broadcast_to(recip_b[rows, :1], (T, PATS))
            lam[rows, :] = (cot[rows, :].astype(F32) * recip).astype(BF16)

    def clear_band():
        for i in range(ROWT):
            for j in range(K):
                if j < i or j > i + 4:
                    band[i * T : (i + 1) * T, j * T : (j + 1) * T] = jnp.zeros((T, T), BF16)

    def across(by, m, source):
        slot = tiles.at[at_x(source, c) * ROWT + m]
        return remote(
            slot, slot, across_s.at[by - 1, m], across_r.at[by - 1, m], n, at_x(by + source, c)
        )

    def relay(by, m):
        slot = tiles.at[at_x(-by, c) * ROWT + m]
        send(None, remote(slot, slot, core_s.at[by, m], core_r.at[by, m], n, mate))

    def share_tiles():
        for m in range(ROWT):
            only(route_if[m], route[m].wait_recv)
            for by in (1, 3):
                send(None, across(by, m, 0))
            relay(0, m)

    def relay_tiles():
        for m in range(ROWT):
            for by in (1, 3) if m < 2 else (3, 1):
                across(by, m, -by).wait_recv()
                if (m < 2) == (by == 1):
                    send(None, across(2, m, -by))
                relay(by, m)
        for m in (0, 2, 1, 3):
            across(2, m, -2).wait_recv()
            relay(2, m)

    def wait_tiles():
        for m in range(ROWT):
            for by in (0, 1, 3, 2):
                slot = tiles.at[at_x(-by, 1 - c) * ROWT + m]
                remote(slot, slot, core_s.at[by, m], core_r.at[by, m], n, mate).wait_recv()

    def tile_of(i, k):
        owner = place[0, i * K + k]
        m = lax.rem(y - owner // NZ + NY, NY)
        lane = lax.rem(z - lax.rem(owner, NZ) - 2 * m + 4 * NZ, NZ)
        return tiles[lane * ROWT + m].astype(F32)

    def fill(i, d):
        total = jnp.zeros((T, T), F32)
        for k in range(K):
            total += tile_of(i, k) * (offsets[i, k] == d).astype(F32)
        band[i * T : (i + 1) * T, (i + d) * T : (i + d + 1) * T] = total.astype(BF16)

    first = ((0, 0), (0, 1), (1, 0), (2, 4), (3, 3), (3, 4))

    def fill_first():
        for i, d in first:
            fill(i, d)

    def fill_rest():
        for i in range(ROWT):
            for d in range(5):
                if (i, d) not in first:
                    fill(i, d)

    back_down = [
        remote(psend.at[0, q], precv.at[1, q], back_s.at[0, q], back_r.at[1, q], n - 1, g)
        for q in range(CHUNKS)
    ]
    back_up = [
        remote(psend.at[1, q], precv.at[0, q], back_s.at[1, q], back_r.at[0, q], n + 1, g)
        for q in range(CHUNKS)
    ]

    def send_back():
        for q in range(CHUNKS):
            cols = slice(q * COLS, (q + 1) * COLS)
            psend[0, q] = dot(
                band[0:HALO, 0:HALO], lam[0:HALO, cols], ((0,), (0,))
            ).astype(BF16)
            psend[1, q] = dot(
                band[HALO:ROWS, 3 * HALO :], lam[HALO:ROWS, cols], ((0,), (0,))
            ).astype(BF16)
            send(has_low, back_down[q])
            send(has_high, back_up[q])

    def outer_products():
        for half in (0, 1):

            def outer(jb, carry, half=half):
                start = pl.multiple_of(half * HALO + jb * HALO, HALO)
                block = dot(
                    lam[half * HALO : (half + 1) * HALO, :],
                    vpad[pl.ds(start, HALO), :],
                    ((1,), (1,)),
                )
                for ii in (0, 1):
                    for jj in (0, 1):
                        gsum[(2 * half + ii) * 6 + 2 * jb + jj] = (
                            block[ii * T : (ii + 1) * T, jj * T : (jj + 1) * T] * -scale
                        )
                return carry

            lax.fori_loop(0, 3, outer, 0)

    def share(i, k):
        return gsum[i * 6 + i % 2 + offsets[i, k]]

    pair = [
        remote(asend.at[by], arecv.at[by], pair_s.at[by], pair_r.at[by], n, mate)
        for by in range(NX)
    ]

    def send_pair():
        for by in (2, 1, 3, 0):
            for i in range(ROWT):
                asend[by, i] = share(i, at_x(by, 1 - c)).astype(BF16)
            send(None, pair[by])

    def forward():
        def step(q, carry):
            cols = pl.ds(pl.multiple_of(q * COLS, COLS), COLS)
            for half in (0, 1):
                rows = slice(half * HALO, (half + 1) * HALO)
                coupled = dot(
                    band[rows, half * HALO : half * HALO + 3 * HALO],
                    vpad[half * HALO : half * HALO + 3 * HALO, cols],
                    ((1,), (0,)),
                )
                for s in range(COLS // T):
                    part = pl.ds(pl.multiple_of(q * COLS + s * T, T), T)
                    source = drive_b[rows, :] * (state[rows, part].astype(F32) - 1.0)
                    resp[rows, part] = (
                        source - coupled[:, s * T : (s + 1) * T]
                    ) * recip_b[rows, :]
            return carry

        lax.fori_loop(0, CHUNKS, step, 0)

    half = ROWT // 2
    hop = [
        remote(
            hsend.at[side], hrecv.at[side], hop_s.at[side], hop_r.at[side], n, at_x((1, 3)[side], c)
        )
        for side in (0, 1)
    ]
    grad = [
        [
            remote(
                bsend.at[side, pl.ds(part * half, half)],
                brecv.at[side, pl.ds(part * half, half)],
                grad_s.at[side, part],
                grad_r.at[side, part],
                n,
                at_x((1, 3)[side], c),
            )
            for part in (0, 1)
        ]
        for side in (0, 1)
    ]

    def summed(by, i):
        return share(i, at_x(by, c)) + arecv[by, i].astype(F32)

    def send_hop():
        pair[2].wait_recv()
        for side in (0, 1):
            for i in range(half):
                hsend[side, i] = summed(2, side * half + i).astype(BF16)
            send(None, hop[side])

    def send_grad():
        for side in (0, 1):
            by = (1, 3)[side]
            pair[by].wait_recv()
            part = 1 - side
            for i in range(part * half, (part + 1) * half):
                bsend[side, i] = summed(by, i).astype(BF16)
            send(None, grad[side][part])

    def send_rest():
        for side in (0, 1):
            by = (1, 3)[side]
            hop[side].wait_recv()
            for i in range(half):
                bsend[side, side * half + i] = (
                    summed(by, side * half + i) + hrecv[side, i].astype(F32)
                ).astype(BF16)
            send(None, grad[side][side])

    def backward():
        def step(q, carry):
            cols = pl.ds(pl.multiple_of(q * COLS, COLS), COLS)
            for half in (0, 1):
                rows = slice(half * HALO, (half + 1) * HALO)
                back = dot(
                    band[:, HALO + half * HALO : 2 * HALO + half * HALO],
                    lam[:, cols],
                    ((0,), (0,)),
                )
                for s in range(COLS // T):
                    part = pl.ds(pl.multiple_of(q * COLS + s * T, T), T)
                    sgrad[rows, part] = (
                        cot[rows, part].astype(F32) - back[:, s * T : (s + 1) * T]
                    ) * recip_b[rows, :]
            return carry

        lax.fori_loop(0, CHUNKS, step, 0)

    def finish_grad():
        pair[0].wait_recv()
        for i in range(ROWT):
            if i % half == 0:
                for side in (0, 1):
                    grad[side][i // half].wait_recv()
            total = summed(0, i)
            for side in (0, 1):
                total += brecv[side, i].astype(F32)
            tgrad[0, i] = total

    def add(side, q):
        rows = slice(side * HALO, (side + 1) * HALO)
        for s in range(COLS // T):
            part = slice(q * COLS + s * T, q * COLS + (s + 1) * T)
            terms = precv[side, q, :, s * T : (s + 1) * T].astype(F32)
            sgrad[rows, part] -= terms * recip_b[rows, :]

    def finish_back():
        for q in range(CHUNKS):

            @pl.when(has_low)
            def _(q=q):
                back_up[q].wait_recv()
                add(0, q)

            @pl.when(has_high)
            def _(q=q):
                back_down[q].wait_recv()
                add(1, q)

    def drain():
        for condition, copy in sent:
            only(condition, copy.wait_send)

    stage_tiles()
    make_volt()
    enter()
    send_tiles()
    send_volt()
    make_lam()
    clear_band()
    share_tiles()
    relay_tiles()
    wait_tiles()
    fill_first()
    send_back()
    fill_rest()
    wait_volt()
    outer_products()
    send_pair()
    forward()
    send_hop()
    send_grad()
    backward()
    send_rest()
    finish_grad()
    finish_back()
    drain()


def write_out(resp, sgrad, tgrad, resp_hbm, sgrad_hbm, tgrad_hbm, sem):
    copies = [
        pltpu.make_async_copy(src, dst, sem.at[i])
        for i, (src, dst) in enumerate(
            ((resp, resp_hbm), (sgrad, sgrad_hbm), (tgrad, tgrad_hbm))
        )
    ]
    for copy in copies:
        copy.start()
    for copy in copies:
        copy.wait()


def body(tile_store, send_order, place, offsets, state, drive, conduct, cotangent):
    groups = lax.axis_size("pat")
    scale = 1.0 / float(PATS * groups) ** 0.5
    vmem = pl.BlockSpec(memory_space=pltpu.VMEM)
    hbm = pl.BlockSpec(memory_space=pltpu.HBM)
    dma = pltpu.SemaphoreType.DMA

    def run(*refs):
        kernel(scale, *refs)

    held = pl.pallas_call(
        run,
        out_shape=(
            jax.ShapeDtypeStruct((ROWS, PATS), F32),
            jax.ShapeDtypeStruct((ROWS, PATS), F32),
            jax.ShapeDtypeStruct((1, ROWT, T, T), F32),
        ),
        in_specs=[hbm] * 8,
        out_specs=(vmem, vmem, vmem),
        scratch_shapes=[
            pltpu.VMEM((ROWT, T), F32),
            pltpu.VMEM((ROWT, T), F32),
            pltpu.SMEM((1, NET), jnp.int32),
            pltpu.SMEM((1, NET), jnp.int32),
            pltpu.SMEM((ROWT, K), jnp.int32),
            pltpu.VMEM((NET, T, T), BF16),
            pltpu.VMEM((ROWT, T, T), BF16),
            pltpu.VMEM((NET, T, T), BF16),
            pltpu.VMEM((ROWS, PATS), jnp.int32),
            pltpu.VMEM((ROWS, PATS), BF16),
            pltpu.VMEM((ROWS + 2 * HALO, PATS), BF16),
            pltpu.VMEM((ROWS, PATS), BF16),
            pltpu.VMEM((ROWS, ROWS + 2 * HALO), BF16),
            pltpu.VMEM((ROWS, T), F32),
            pltpu.VMEM((ROWS, T), F32),
            pltpu.VMEM((2, CHUNKS, HALO, COLS), BF16),
            pltpu.VMEM((2, CHUNKS, HALO, COLS), BF16),
            pltpu.VMEM((24, T, T), F32),
            pltpu.VMEM((NX, ROWT, T, T), BF16),
            pltpu.VMEM((NX, ROWT, T, T), BF16),
            pltpu.VMEM((2, ROWT // 2, T, T), BF16),
            pltpu.VMEM((2, ROWT // 2, T, T), BF16),
            pltpu.VMEM((2, ROWT, T, T), BF16),
            pltpu.VMEM((2, ROWT, T, T), BF16),
            dma((14,)),
            dma((ROWT,)),
            dma((ROWT,)),
            dma((4,)),
            dma((4,)),
            dma((3, ROWT)),
            dma((3, ROWT)),
            dma((4, ROWT)),
            dma((4, ROWT)),
            dma((2, CHUNKS)),
            dma((2, CHUNKS)),
            dma((NX,)),
            dma((NX,)),
            dma((2,)),
            dma((2,)),
            dma((2, 2)),
            dma((2, 2)),
        ],
        compiler_params=pltpu.CompilerParams(
            collective_id=0, has_side_effects=True, vmem_limit_bytes=40 * 1024 * 1024
        ),
        name="crosstalk",
    )(
        *[
            pltpu.with_memory_space_constraint(value, pltpu.HBM)
            for value in (
                drive.reshape(ROWT, T),
                conduct.reshape(ROWT, T),
                send_order,
                place,
                offsets,
                tile_store,
                state,
                cotangent,
            )
        ],
    )

    return pl.pallas_call(
        write_out,
        out_shape=[jax.ShapeDtypeStruct(value.shape, value.dtype) for value in held],
        in_specs=[vmem] * 3,
        out_specs=[hbm] * 3,
        scratch_shapes=[dma((3,))],
        compiler_params=pltpu.CompilerParams(vmem_limit_bytes=1024 * 1024),
        name="write_out",
    )(*held)


def solution(mesh):
    placed = (
        P("net", None, None),
        P("net", None),
        P("net", None),
        P("net", None),
        P("net", "pat"),
        P("net"),
        P("net"),
        P("net", "pat"),
    )
    return jax.shard_map(
        body,
        mesh=mesh,
        in_specs=placed,
        out_specs=(P("net", "pat"), P("net", "pat"), P("pat", "net", None, None)),
        check_vma=False,
    )
```

```python
import jax
import jax.numpy as jnp
from jax import lax
from jax.experimental import pallas as pl
from jax.experimental.pallas import tpu as pltpu
from jax.sharding import PartitionSpec as P

MESH = pl.DeviceIdType.MESH
BF16 = jnp.bfloat16
F32 = jnp.float32
T = 128
ROWT = 4
K = 8
ROWS = 512
PATS = 1024
HALO = 256
NET = 32
NZ = 8
NY = 4
NX = 4
COLS = 256
CHUNKS = PATS // COLS


def mod(value, size):
    return lax.rem(value + 4 * size, size)


def dot(a, b, dims):
    return lax.dot_general(a, b, (dims, ((), ())), preferred_element_type=F32)


def kernel(
    scale,
    drive_hbm,
    conduct_hbm,
    order_hbm,
    place_hbm,
    offsets_hbm,
    store_hbm,
    state_hbm,
    cot_hbm,
    resp,
    sgrad,
    tgrad,
    drive,
    conduct,
    order,
    place,
    offsets,
    store,
    stage,
    tiles,
    state,
    cot,
    vpad,
    lam,
    band,
    drive_b,
    recip_b,
    psend,
    precv,
    gsum,
    asend,
    arecv,
    hsend,
    hrecv,
    bsend,
    brecv,
    load_sem,
    route_s,
    route_r,
    volt_s,
    volt_r,
    across_s,
    across_r,
    core_s,
    core_r,
    back_s,
    back_r,
    pair_s,
    pair_r,
    hop_s,
    hop_r,
    grad_s,
    grad_r,
):
    n = lax.axis_index("net")
    g = lax.axis_index("pat")
    y, z = n // NZ, lax.rem(n, NZ)
    x, c = g // 2, lax.rem(g, 2)
    mate = g + 1 - 2 * c

    def at_x(by, core):
        return mod(x + by, NX) * 2 + core

    def remote(src, dst, send, recv, net, pat):
        return pltpu.make_async_remote_copy(
            src_ref=src,
            dst_ref=dst,
            send_sem=send,
            recv_sem=recv,
            device_id=(net, pat),
            device_id_type=MESH,
        )

    barrier = pltpu.get_barrier_semaphore()

    def greet(net, pat):
        pl.semaphore_signal(barrier, inc=1, device_id=(net, pat), device_id_type=MESH)

    def source_net(m):
        return mod(y - m, NY) * NZ + mod(z - g - 2 * m, NZ)

    def target_net(m):
        return mod(y + m, NY) * NZ + mod(z + g + 2 * m, NZ)

    for m in (1, 2, 3):
        greet(source_net(m), g)

    @pl.when(g != 0)
    def _():
        greet(source_net(0), g)

    for by in (1, 3):
        greet(n, at_x(by, c))
    greet(n, mate)

    @pl.when(n > 0)
    def _():
        greet(n - 1, g)

    @pl.when(n < NET - 1)
    def _():
        greet(n + 1, g)

    loads = []
    for r in (0, 3, 1, 2):
        rows = pl.ds(r * T, T)
        loads.append(
            pltpu.make_async_copy(state_hbm.at[rows], state.at[rows], load_sem.at[r])
        )
    store_load = pltpu.make_async_copy(store_hbm, store, load_sem.at[8])
    cot_loads = []
    for r in range(ROWT):
        rows = pl.ds(r * T, T)
        cot_loads.append(
            pltpu.make_async_copy(cot_hbm.at[rows], cot.at[rows], load_sem.at[4 + r])
        )
    small = [
        pltpu.make_async_copy(drive_hbm, drive, load_sem.at[9]),
        pltpu.make_async_copy(conduct_hbm, conduct, load_sem.at[10]),
        pltpu.make_async_copy(order_hbm, order, load_sem.at[11]),
        pltpu.make_async_copy(place_hbm, place, load_sem.at[12]),
        pltpu.make_async_copy(offsets_hbm, offsets, load_sem.at[13]),
    ]
    for copy in small + loads[:2] + [store_load] + loads[2:] + cot_loads:
        copy.start()
    for copy in small:
        copy.wait()

    eye = lax.broadcasted_iota(jnp.int32, (T, T), 0) == lax.broadcasted_iota(
        jnp.int32, (T, T), 1
    )
    ratio = []
    for r in range(ROWT):
        d_row = jnp.broadcast_to(drive[r : r + 1, :], (T, T))
        g_row = jnp.broadcast_to(conduct[r : r + 1, :], (T, T))
        d_col = jnp.sum(jnp.where(eye, d_row, 0.0), axis=1, keepdims=True)
        g_col = jnp.sum(jnp.where(eye, g_row, 0.0), axis=1, keepdims=True)
        drive_b[r * T : (r + 1) * T, :] = jnp.broadcast_to(d_col, (T, T))
        recip_b[r * T : (r + 1) * T, :] = jnp.broadcast_to(1.0 / g_col, (T, T))
        ratio.append((d_col / g_col).astype(BF16).astype(F32))

    sent = []

    def only(condition, act):
        if condition is None:
            act()
        else:
            pl.when(condition)(act)

    def send(condition, copy):
        only(condition, copy.start)
        sent.append((condition, copy))

    has_low, has_high = n > 0, n < NET - 1

    def stage_tiles():
        store_load.wait()
        for t in range(ROWT):
            stage[t] = store[order[0, target_net(nth(t, x))]]

        @pl.when(g == 0)
        def _():
            tiles[0] = store[order[0, n]]

    def make_volt(which):
        for at in which:
            r = (0, 3, 1, 2)[at]
            loads[at].wait()
            rows = slice(r * T, (r + 1) * T)
            levels = state[rows, :].astype(F32) - 1.0
            vpad[HALO + r * T : HALO + (r + 1) * T, :] = (levels * ratio[r]).astype(BF16)

    def clear_ends():
        @pl.when(n == 0)
        def _():
            vpad[0:HALO, :] = jnp.zeros((HALO, PATS), BF16)

        @pl.when(n == NET - 1)
        def _():
            vpad[HALO + ROWS :, :] = jnp.zeros((HALO, PATS), BF16)

    def enter():
        peers = (
            6
            + jnp.where(g != 0, 1, 0)
            + jnp.where(n > 0, 1, 0)
            + jnp.where(n < NET - 1, 1, 0)
        )
        pl.semaphore_wait(barrier, peers)

    def nth(t, chip):
        return jnp.where(chip < 2, (0, 3, 1, 2)[t], (1, 0, 2, 3)[t])

    def route(t):
        m = nth(t, x)
        return remote(
            stage.at[t],
            tiles.at[g * ROWT + m],
            route_s.at[t],
            route_r.at[t],
            target_net(m),
            g,
        )

    routes = [route(t) for t in range(ROWT)]
    route_if = [g != 0, None, None, None]

    def send_tiles():
        for t in (3, 2, 1, 0):
            send(route_if[t], routes[t])

    volt_down, volt_up = [], []
    for h in (0, 1):
        volt_down.append(
            remote(
                vpad.at[pl.ds(HALO + h * T, T)],
                vpad.at[pl.ds(HALO + ROWS + h * T, T)],
                volt_s.at[h],
                volt_r.at[h],
                n - 1,
                g,
            )
        )
        volt_up.append(
            remote(
                vpad.at[pl.ds(ROWS + h * T, T)],
                vpad.at[pl.ds(h * T, T)],
                volt_s.at[2 + h],
                volt_r.at[2 + h],
                n + 1,
                g,
            )
        )

    def send_outer():
        send(has_low, volt_down[0])
        send(has_high, volt_up[1])

    def send_inner():
        send(has_low, volt_down[1])
        send(has_high, volt_up[0])

    def wait_volt():
        for h in (0, 1):
            only(has_low, volt_up[h].wait_recv)
            only(has_high, volt_down[h].wait_recv)

    def make_lam():
        for r in range(ROWT):
            cot_loads[r].wait()
            rows = slice(r * T, (r + 1) * T)
            recip = jnp.broadcast_to(recip_b[rows, :1], (T, PATS))
            lam[rows, :] = (cot[rows, :].astype(F32) * recip).astype(BF16)

    def clear_band():
        for i in range(ROWT):
            for j in range(K):
                if j < i or j > i + 4:
                    band[i * T : (i + 1) * T, j * T : (j + 1) * T] = jnp.zeros((T, T), BF16)

    def slot_of(by, core, t):
        chip = mod(x + by, NX)
        return tiles.at[(chip * 2 + core) * ROWT + nth(t, chip)]

    def across(by, t, source):
        slot = slot_of(source, c, t)
        return remote(
            slot, slot, across_s.at[by - 1, t], across_r.at[by - 1, t], n, at_x(by + source, c)
        )

    def relay(by, t, core):
        slot = slot_of(-by, core, t)
        return remote(slot, slot, core_s.at[by, t], core_r.at[by, t], n, mate)

    def share_tiles():
        for t in range(ROWT):
            only(route_if[t], routes[t].wait_recv)
            for by in (1, 3):
                send(None, across(by, t, 0))
            send(None, relay(0, t, c))

    def relay_tiles():
        for t in range(ROWT):
            for by in (1, 3) if t in (0, 3) else (3, 1):
                across(by, t, -by).wait_recv()
                if (t in (0, 3)) == (by == 1):
                    send(None, across(2, t, -by))
                send(None, relay(by, t, c))
        for t in range(ROWT):
            across(2, t, -2).wait_recv()
            send(None, relay(2, t, c))

    def wait_tiles():
        for by in (0, 1, 3, 2):
            for t in range(ROWT):
                relay(by, t, 1 - c).wait_recv()

    def tile_of(i, k):
        owner = place[0, i * K + k]
        m = lax.rem(y - owner // NZ + NY, NY)
        lane = lax.rem(z - lax.rem(owner, NZ) - 2 * m + 4 * NZ, NZ)
        return tiles[lane * ROWT + m].astype(F32)

    def fill(i, d):
        total = jnp.zeros((T, T), F32)
        for k in range(K):
            total += tile_of(i, k) * (offsets[i, k] == d).astype(F32)
        band[i * T : (i + 1) * T, (i + d) * T : (i + d + 1) * T] = total.astype(BF16)

    first = ((0, 0), (0, 1), (1, 0), (2, 4), (3, 3), (3, 4))

    def fill_first():
        for i, d in first:
            fill(i, d)

    def fill_rest():
        for i in range(ROWT):
            for d in range(5):
                if (i, d) not in first:
                    fill(i, d)

    back_down = [
        remote(psend.at[0, q], precv.at[1, q], back_s.at[0, q], back_r.at[1, q], n - 1, g)
        for q in range(CHUNKS)
    ]
    back_up = [
        remote(psend.at[1, q], precv.at[0, q], back_s.at[1, q], back_r.at[0, q], n + 1, g)
        for q in range(CHUNKS)
    ]

    def send_back():
        low = jnp.transpose(band[0:HALO, 0:HALO])
        high = jnp.transpose(band[HALO:ROWS, 3 * HALO :])
        for q in range(CHUNKS):
            cols = slice(q * COLS, (q + 1) * COLS)
            psend[0, q] = dot(low, lam[0:HALO, cols], ((1,), (0,))).astype(BF16)
            psend[1, q] = dot(high, lam[HALO:ROWS, cols], ((1,), (0,))).astype(BF16)
            send(has_low, back_down[q])
            send(has_high, back_up[q])

    def outer(half, jb):
        start = half * HALO + jb * HALO
        block = dot(
            lam[half * HALO : (half + 1) * HALO, :],
            vpad[start : start + HALO, :],
            ((1,), (1,)),
        )
        for ii in (0, 1):
            for jj in (0, 1):
                gsum[(2 * half + ii) * 6 + 2 * jb + jj] = (
                    block[ii * T : (ii + 1) * T, jj * T : (jj + 1) * T] * -scale
                )

    def outer_own():
        for half, jb in ((0, 1), (0, 2), (1, 0), (1, 1)):
            outer(half, jb)

    def outer_halo():
        outer(0, 0)
        outer(1, 2)

    def share(i, k):
        return gsum[i * 6 + i % 2 + offsets[i, k]]

    pair = [
        remote(asend.at[by], arecv.at[by], pair_s.at[by], pair_r.at[by], n, mate)
        for by in range(NX)
    ]

    def send_pair():
        for by in (2, 1, 3, 0):
            for i in range(ROWT):
                asend[by, i] = share(i, at_x(by, 1 - c)).astype(BF16)
            send(None, pair[by])

    def forward():
        def step(q, carry):
            cols = pl.ds(pl.multiple_of(q * COLS, COLS), COLS)
            for half in (0, 1):
                rows = slice(half * HALO, (half + 1) * HALO)
                coupled = dot(
                    band[rows, half * HALO : half * HALO + 3 * HALO],
                    vpad[half * HALO : half * HALO + 3 * HALO, cols],
                    ((1,), (0,)),
                )
                for s in range(COLS // T):
                    part = pl.ds(pl.multiple_of(q * COLS + s * T, T), T)
                    source = drive_b[rows, :] * (state[rows, part].astype(F32) - 1.0)
                    resp[rows, part] = (
                        source - coupled[:, s * T : (s + 1) * T]
                    ) * recip_b[rows, :]
            return carry

        lax.fori_loop(0, CHUNKS, step, 0)

    half = ROWT // 2
    hop = [
        remote(
            hsend.at[side], hrecv.at[side], hop_s.at[side], hop_r.at[side], n, at_x((1, 3)[side], c)
        )
        for side in (0, 1)
    ]
    grad = [
        [
            remote(
                bsend.at[side, pl.ds(part * half, half)],
                brecv.at[side, pl.ds(part * half, half)],
                grad_s.at[side, part],
                grad_r.at[side, part],
                n,
                at_x((1, 3)[side], c),
            )
            for part in (0, 1)
        ]
        for side in (0, 1)
    ]

    def summed(by, i):
        return share(i, at_x(by, c)) + arecv[by, i].astype(F32)

    def send_hop():
        pair[2].wait_recv()
        for side in (0, 1):
            for i in range(half):
                hsend[side, i] = summed(2, side * half + i).astype(BF16)
            send(None, hop[side])

    def send_grad():
        for side in (0, 1):
            by = (1, 3)[side]
            pair[by].wait_recv()
            part = 1 - side
            for i in range(part * half, (part + 1) * half):
                bsend[side, i] = summed(by, i).astype(BF16)
            send(None, grad[side][part])

    def send_rest():
        for side in (0, 1):
            by = (1, 3)[side]
            hop[side].wait_recv()
            for i in range(half):
                bsend[side, side * half + i] = (
                    summed(by, side * half + i) + hrecv[side, i].astype(F32)
                ).astype(BF16)
            send(None, grad[side][side])

    def backward():
        def step(q, carry):
            cols = pl.ds(pl.multiple_of(q * COLS, COLS), COLS)
            for half in (0, 1):
                rows = slice(half * HALO, (half + 1) * HALO)
                back = dot(
                    band[:, HALO + half * HALO : 2 * HALO + half * HALO],
                    lam[:, cols],
                    ((0,), (0,)),
                )
                for s in range(COLS // T):
                    part = pl.ds(pl.multiple_of(q * COLS + s * T, T), T)
                    sgrad[rows, part] = (
                        cot[rows, part].astype(F32) - back[:, s * T : (s + 1) * T]
                    ) * recip_b[rows, :]
            return carry

        lax.fori_loop(0, CHUNKS, step, 0)

    def finish_grad():
        pair[0].wait_recv()
        for i in range(ROWT):
            if i % half == 0:
                for side in (0, 1):
                    grad[side][i // half].wait_recv()
            total = summed(0, i)
            for side in (0, 1):
                total += brecv[side, i].astype(F32)
            tgrad[0, i] = total

    def add(side, q):
        rows = slice(side * HALO, (side + 1) * HALO)
        for s in range(COLS // T):
            part = slice(q * COLS + s * T, q * COLS + (s + 1) * T)
            terms = precv[side, q, :, s * T : (s + 1) * T].astype(F32)
            sgrad[rows, part] -= terms * recip_b[rows, :]

    def finish_back():
        for q in range(CHUNKS):

            @pl.when(has_low)
            def _(q=q):
                back_up[q].wait_recv()
                add(0, q)

            @pl.when(has_high)
            def _(q=q):
                back_down[q].wait_recv()
                add(1, q)

    def drain():
        for condition, copy in sent:
            only(condition, copy.wait_send)

    stage_tiles()
    make_volt((0, 1))
    enter()
    send_tiles()
    send_outer()
    make_volt((2, 3))
    send_inner()
    make_lam()
    clear_band()
    clear_ends()
    outer_own()
    share_tiles()
    relay_tiles()
    wait_tiles()
    fill_first()
    send_back()
    wait_volt()
    outer_halo()
    send_pair()
    fill_rest()
    forward()
    send_hop()
    send_grad()
    backward()
    send_rest()
    finish_grad()
    finish_back()
    drain()


def write_out(resp, sgrad, tgrad, resp_hbm, sgrad_hbm, tgrad_hbm, sem):
    copies = [pltpu.make_async_copy(tgrad, tgrad_hbm, sem.at[0])]
    for r in range(ROWT):
        rows = pl.ds(r * T, T)
        copies += [
            pltpu.make_async_copy(resp.at[rows], resp_hbm.at[rows], sem.at[1 + r]),
            pltpu.make_async_copy(sgrad.at[rows], sgrad_hbm.at[rows], sem.at[5 + r]),
        ]
    for copy in copies:
        copy.start()
    for copy in copies:
        copy.wait()


def body(tile_store, send_order, place, offsets, state, drive, conduct, cotangent):
    groups = lax.axis_size("pat")
    scale = 1.0 / float(PATS * groups) ** 0.5
    vmem = pl.BlockSpec(memory_space=pltpu.VMEM)
    hbm = pl.BlockSpec(memory_space=pltpu.HBM)
    dma = pltpu.SemaphoreType.DMA

    def run(*refs):
        kernel(scale, *refs)

    held = pl.pallas_call(
        run,
        out_shape=(
            jax.ShapeDtypeStruct((ROWS, PATS), F32),
            jax.ShapeDtypeStruct((ROWS, PATS), F32),
            jax.ShapeDtypeStruct((1, ROWT, T, T), F32),
        ),
        in_specs=[hbm] * 8,
        out_specs=(vmem, vmem, vmem),
        scratch_shapes=[
            pltpu.VMEM((ROWT, T), F32),
            pltpu.VMEM((ROWT, T), F32),
            pltpu.SMEM((1, NET), jnp.int32),
            pltpu.SMEM((1, NET), jnp.int32),
            pltpu.SMEM((ROWT, K), jnp.int32),
            pltpu.VMEM((NET, T, T), BF16),
            pltpu.VMEM((ROWT, T, T), BF16),
            pltpu.VMEM((NET, T, T), BF16),
            pltpu.VMEM((ROWS, PATS), jnp.int32),
            pltpu.VMEM((ROWS, PATS), BF16),
            pltpu.VMEM((ROWS + 2 * HALO, PATS), BF16),
            pltpu.VMEM((ROWS, PATS), BF16),
            pltpu.VMEM((ROWS, ROWS + 2 * HALO), BF16),
            pltpu.VMEM((ROWS, T), F32),
            pltpu.VMEM((ROWS, T), F32),
            pltpu.VMEM((2, CHUNKS, HALO, COLS), BF16),
            pltpu.VMEM((2, CHUNKS, HALO, COLS), BF16),
            pltpu.VMEM((24, T, T), F32),
            pltpu.VMEM((NX, ROWT, T, T), BF16),
            pltpu.VMEM((NX, ROWT, T, T), BF16),
            pltpu.VMEM((2, ROWT // 2, T, T), BF16),
            pltpu.VMEM((2, ROWT // 2, T, T), BF16),
            pltpu.VMEM((2, ROWT, T, T), BF16),
            pltpu.VMEM((2, ROWT, T, T), BF16),
            dma((14,)),
            dma((ROWT,)),
            dma((ROWT,)),
            dma((4,)),
            dma((4,)),
            dma((3, ROWT)),
            dma((3, ROWT)),
            dma((4, ROWT)),
            dma((4, ROWT)),
            dma((2, CHUNKS)),
            dma((2, CHUNKS)),
            dma((NX,)),
            dma((NX,)),
            dma((2,)),
            dma((2,)),
            dma((2, 2)),
            dma((2, 2)),
        ],
        compiler_params=pltpu.CompilerParams(
            collective_id=0, has_side_effects=True, vmem_limit_bytes=40 * 1024 * 1024
        ),
        name="crosstalk",
    )(
        *[
            pltpu.with_memory_space_constraint(value, pltpu.HBM)
            for value in (
                drive.reshape(ROWT, T),
                conduct.reshape(ROWT, T),
                send_order,
                place,
                offsets,
                tile_store,
                state,
                cotangent,
            )
        ],
    )

    return pl.pallas_call(
        write_out,
        out_shape=[jax.ShapeDtypeStruct(value.shape, value.dtype) for value in held],
        in_specs=[vmem] * 3,
        out_specs=[hbm] * 3,
        scratch_shapes=[dma((9,))],
        compiler_params=pltpu.CompilerParams(vmem_limit_bytes=1024 * 1024),
        name="write_out",
    )(*held)


def solution(mesh):
    placed = (
        P("net", None, None),
        P("net", None),
        P("net", None),
        P("net", None),
        P("net", "pat"),
        P("net"),
        P("net"),
        P("net", "pat"),
    )
    return jax.shard_map(
        body,
        mesh=mesh,
        in_specs=placed,
        out_specs=(P("net", "pat"), P("net", "pat"), P("pat", "net", None, None)),
        check_vma=False,
    )
```

```python
import jax
import jax.numpy as jnp
from jax import lax
from jax.experimental import pallas as pl
from jax.experimental.pallas import tpu as pltpu
from jax.sharding import PartitionSpec as P

MESH = pl.DeviceIdType.MESH
BF16 = jnp.bfloat16
F32 = jnp.float32
T = 128
ROWT = 4
K = 8
ROWS = 512
PATS = 1024
HALO = 256
NET = 32
NZ = 8
NY = 4
NX = 4
COLS = 256
CHUNKS = PATS // COLS
EARLY = 1


def mod(value, size):
    return lax.rem(value + 4 * size, size)


def dot(a, b, dims):
    return lax.dot_general(a, b, (dims, ((), ())), preferred_element_type=F32)


def kernel(
    scale,
    drive_hbm,
    conduct_hbm,
    order_hbm,
    place_hbm,
    offsets_hbm,
    store_hbm,
    state_hbm,
    cot_hbm,
    resp,
    sgrad,
    tgrad,
    drive,
    conduct,
    order,
    place,
    offsets,
    store,
    stage,
    tiles,
    state,
    cot,
    vpad,
    lam,
    band,
    drive_b,
    recip_b,
    psend,
    precv,
    lamx,
    corner,
    gsum,
    asend,
    arecv,
    hsend,
    hrecv,
    bsend,
    brecv,
    load_sem,
    route_s,
    route_r,
    volt_s,
    volt_r,
    across_s,
    across_r,
    core_s,
    core_r,
    back_s,
    back_r,
    lams_s,
    lams_r,
    corner_s,
    corner_r,
    twin_s,
    twin_r,
    pair_s,
    pair_r,
    hop_s,
    hop_r,
    grad_s,
    grad_r,
):
    n = lax.axis_index("net")
    g = lax.axis_index("pat")
    y, z = n // NZ, lax.rem(n, NZ)
    x, c = g // 2, lax.rem(g, 2)
    mate = g + 1 - 2 * c

    def at_x(by, core):
        return mod(x + by, NX) * 2 + core

    def remote(src, dst, send, recv, net, pat):
        return pltpu.make_async_remote_copy(
            src_ref=src,
            dst_ref=dst,
            send_sem=send,
            recv_sem=recv,
            device_id=(net, pat),
            device_id_type=MESH,
        )

    barrier = pltpu.get_barrier_semaphore()

    def greet(net, pat):
        pl.semaphore_signal(barrier, inc=1, device_id=(net, pat), device_id_type=MESH)

    def source_net(m):
        return mod(y - m, NY) * NZ + mod(z - g - 2 * m, NZ)

    def target_net(m):
        return mod(y + m, NY) * NZ + mod(z + g + 2 * m, NZ)

    for m in (1, 2, 3):
        greet(source_net(m), g)

    @pl.when(g != 0)
    def _():
        greet(source_net(0), g)

    for by in (1, 3):
        greet(n, at_x(by, c))
    greet(n, mate)

    @pl.when(n > 0)
    def _():
        greet(n - 1, g)

    @pl.when(n < NET - 1)
    def _():
        greet(n + 1, g)

    loads = []
    for r in (0, 3, 1, 2):
        rows = pl.ds(r * T, T)
        loads.append(
            pltpu.make_async_copy(state_hbm.at[rows], state.at[rows], load_sem.at[r])
        )
    store_load = pltpu.make_async_copy(store_hbm, store, load_sem.at[8])
    cot_loads = []
    for r in range(ROWT):
        rows = pl.ds(r * T, T)
        cot_loads.append(
            pltpu.make_async_copy(cot_hbm.at[rows], cot.at[rows], load_sem.at[4 + r])
        )
    small = [
        pltpu.make_async_copy(drive_hbm, drive, load_sem.at[9]),
        pltpu.make_async_copy(conduct_hbm, conduct, load_sem.at[10]),
        pltpu.make_async_copy(order_hbm, order, load_sem.at[11]),
        pltpu.make_async_copy(place_hbm, place, load_sem.at[12]),
        pltpu.make_async_copy(offsets_hbm, offsets, load_sem.at[13]),
    ]
    for copy in small + loads[:2] + [store_load] + loads[2:] + cot_loads:
        copy.start()
    for copy in small:
        copy.wait()

    eye = lax.broadcasted_iota(jnp.int32, (T, T), 0) == lax.broadcasted_iota(
        jnp.int32, (T, T), 1
    )
    ratio = []
    for r in range(ROWT):
        d_row = jnp.broadcast_to(drive[r : r + 1, :], (T, T))
        g_row = jnp.broadcast_to(conduct[r : r + 1, :], (T, T))
        d_col = jnp.sum(jnp.where(eye, d_row, 0.0), axis=1, keepdims=True)
        g_col = jnp.sum(jnp.where(eye, g_row, 0.0), axis=1, keepdims=True)
        drive_b[r * T : (r + 1) * T, :] = jnp.broadcast_to(d_col, (T, T))
        recip_b[r * T : (r + 1) * T, :] = jnp.broadcast_to(1.0 / g_col, (T, T))
        ratio.append((d_col / g_col).astype(BF16).astype(F32))

    sent = []

    def only(condition, act):
        if condition is None:
            act()
        else:
            pl.when(condition)(act)

    def send(condition, copy):
        only(condition, copy.start)
        sent.append((condition, copy))

    has_low, has_high = n > 0, n < NET - 1

    def stage_tiles():
        store_load.wait()
        for t in range(ROWT):
            stage[t] = store[order[0, target_net(nth(t, x))]]

        @pl.when(g == 0)
        def _():
            tiles[0] = store[order[0, n]]

    def make_volt(which):
        for at in which:
            r = (0, 3, 1, 2)[at]
            loads[at].wait()
            rows = slice(r * T, (r + 1) * T)
            levels = state[rows, :].astype(F32) - 1.0
            vpad[HALO + r * T : HALO + (r + 1) * T, :] = (levels * ratio[r]).astype(BF16)

    def clear_ends():
        @pl.when(n == 0)
        def _():
            vpad[0:HALO, :] = jnp.zeros((HALO, PATS), BF16)

        @pl.when(n == NET - 1)
        def _():
            vpad[HALO + ROWS :, :] = jnp.zeros((HALO, PATS), BF16)

    def enter():
        peers = (
            6
            + jnp.where(g != 0, 1, 0)
            + jnp.where(n > 0, 1, 0)
            + jnp.where(n < NET - 1, 1, 0)
        )
        pl.semaphore_wait(barrier, peers)

    def nth(t, chip):
        return jnp.where(chip < 2, (0, 3, 1, 2)[t], (1, 0, 2, 3)[t])

    def route(t):
        m = nth(t, x)
        return remote(
            stage.at[t],
            tiles.at[g * ROWT + m],
            route_s.at[t],
            route_r.at[t],
            target_net(m),
            g,
        )

    routes = [route(t) for t in range(ROWT)]
    route_if = [g != 0, None, None, None]

    def send_tiles():
        for t in (3, 2, 1, 0):
            send(route_if[t], routes[t])

    volt_down, volt_up = [], []
    for h in (0, 1):
        volt_down.append(
            remote(
                vpad.at[pl.ds(HALO + h * T, T)],
                vpad.at[pl.ds(HALO + ROWS + h * T, T)],
                volt_s.at[h],
                volt_r.at[h],
                n - 1,
                g,
            )
        )
        volt_up.append(
            remote(
                vpad.at[pl.ds(ROWS + h * T, T)],
                vpad.at[pl.ds(h * T, T)],
                volt_s.at[2 + h],
                volt_r.at[2 + h],
                n + 1,
                g,
            )
        )

    def send_outer():
        send(has_low, volt_down[0])
        send(has_high, volt_up[1])

    def send_inner():
        send(has_low, volt_down[1])
        send(has_high, volt_up[0])

    def wait_volt():
        for h in (0, 1):
            only(has_low, volt_up[h].wait_recv)
            only(has_high, volt_down[h].wait_recv)

    def make_lam():
        for r in range(ROWT):
            cot_loads[r].wait()
            rows = slice(r * T, (r + 1) * T)
            recip = jnp.broadcast_to(recip_b[rows, :1], (T, PATS))
            lam[rows, :] = (cot[rows, :].astype(F32) * recip).astype(BF16)

    def clear_band():
        for i in range(ROWT):
            for j in range(K):
                if j < i or j > i + 4:
                    band[i * T : (i + 1) * T, j * T : (j + 1) * T] = jnp.zeros((T, T), BF16)

    def slot_of(by, core, t):
        chip = mod(x + by, NX)
        return tiles.at[(chip * 2 + core) * ROWT + nth(t, chip)]

    def across(by, t, source):
        slot = slot_of(source, c, t)
        return remote(
            slot, slot, across_s.at[by - 1, t], across_r.at[by - 1, t], n, at_x(by + source, c)
        )

    def relay(by, t, core):
        slot = slot_of(-by, core, t)
        return remote(slot, slot, core_s.at[by, t], core_r.at[by, t], n, mate)

    def share_tiles():
        for t in range(ROWT):
            only(route_if[t], routes[t].wait_recv)
            for by in (1, 3):
                send(None, across(by, t, 0))
            send(None, relay(0, t, c))

    def relay_tiles():
        for t in range(ROWT):
            for by in (1, 3) if t in (0, 3) else (3, 1):
                across(by, t, -by).wait_recv()
                if (t in (0, 3)) == (by == 1):
                    send(None, across(2, t, -by))
                send(None, relay(by, t, c))
        for t in range(ROWT):
            across(2, t, -2).wait_recv()
            send(None, relay(2, t, c))

    def wait_tiles():
        for by in (0, 1, 3, 2):
            for t in range(ROWT):
                relay(by, t, 1 - c).wait_recv()

    def tile_of(i, k):
        owner = place[0, i * K + k]
        m = lax.rem(y - owner // NZ + NY, NY)
        lane = lax.rem(z - lax.rem(owner, NZ) - 2 * m + 4 * NZ, NZ)
        return tiles[lane * ROWT + m].astype(F32)

    def fill(i, d):
        total = jnp.zeros((T, T), F32)
        for k in range(K):
            total += tile_of(i, k) * (offsets[i, k] == d).astype(F32)
        band[i * T : (i + 1) * T, (i + d) * T : (i + d + 1) * T] = total.astype(BF16)

    first = ((0, 0), (0, 1), (1, 0), (2, 4), (3, 3), (3, 4))

    def fill_first():
        for i, d in first:
            fill(i, d)

    def fill_rest():
        for i in range(ROWT):
            for d in range(5):
                if (i, d) not in first:
                    fill(i, d)

    lam_down = [
        remote(
            lam.at[pl.ds(0, HALO), pl.ds(q * COLS, COLS)],
            lamx.at[1, q],
            lams_s.at[0, q],
            lams_r.at[1, q],
            n - 1,
            g,
        )
        for q in range(EARLY)
    ]
    lam_up = [
        remote(
            lam.at[pl.ds(HALO, HALO), pl.ds(q * COLS, COLS)],
            lamx.at[0, q],
            lams_s.at[1, q],
            lams_r.at[0, q],
            n + 1,
            g,
        )
        for q in range(EARLY)
    ]

    def send_lam():
        for q in range(EARLY):
            send(has_low, lam_down[q])
            send(has_high, lam_up[q])

    part = pl.multiple_of(c * T, T)
    corner_down = remote(
        band.at[pl.ds(part, T), pl.ds(0, HALO)],
        corner.at[1, c],
        corner_s.at[0],
        corner_r.at[1],
        n - 1,
        g,
    )
    corner_up = remote(
        band.at[pl.ds(HALO + part, T), pl.ds(3 * HALO, HALO)],
        corner.at[0, c],
        corner_s.at[1],
        corner_r.at[0],
        n + 1,
        g,
    )

    def send_corner():
        send(has_low, corner_down)
        send(has_high, corner_up)

    def twin(side, core):
        return remote(
            corner.at[side, core], corner.at[side, core], twin_s.at[side], twin_r.at[side], n, mate
        )

    def relay_corner():
        only(has_low, corner_up.wait_recv)
        send(has_low, twin(0, c))
        only(has_high, corner_down.wait_recv)
        send(has_high, twin(1, c))

    def finish_lam():
        for side, condition, copies in ((0, has_low, lam_up), (1, has_high, lam_down)):

            @pl.when(condition)
            def _(side=side, copies=copies):
                twin(side, 1 - c).wait_recv()
                rows = slice(side * HALO, (side + 1) * HALO)
                turned = jnp.transpose(corner[side].reshape(HALO, HALO))
                for q in range(EARLY):
                    copies[q].wait_recv()
                    terms = dot(turned, lamx[side, q], ((1,), (0,)))
                    for s in range(COLS // T):
                        at = slice(q * COLS + s * T, q * COLS + (s + 1) * T)
                        sgrad[rows, at] -= terms[:, s * T : (s + 1) * T] * recip_b[rows, :]

    back_down = [
        remote(psend.at[0, q], precv.at[1, q], back_s.at[0, q], back_r.at[1, q], n - 1, g)
        for q in range(CHUNKS)
    ]
    back_up = [
        remote(psend.at[1, q], precv.at[0, q], back_s.at[1, q], back_r.at[0, q], n + 1, g)
        for q in range(CHUNKS)
    ]

    def send_back():
        low = jnp.transpose(band[0:HALO, 0:HALO])
        high = jnp.transpose(band[HALO:ROWS, 3 * HALO :])
        for q in range(EARLY, CHUNKS):
            cols = slice(q * COLS, (q + 1) * COLS)
            psend[0, q] = dot(low, lam[0:HALO, cols], ((1,), (0,))).astype(BF16)
            psend[1, q] = dot(high, lam[HALO:ROWS, cols], ((1,), (0,))).astype(BF16)
            send(has_low, back_down[q])
            send(has_high, back_up[q])

    def outer(half, jb):
        start = half * HALO + jb * HALO
        block = dot(
            lam[half * HALO : (half + 1) * HALO, :],
            vpad[start : start + HALO, :],
            ((1,), (1,)),
        )
        for ii in (0, 1):
            for jj in (0, 1):
                gsum[(2 * half + ii) * 6 + 2 * jb + jj] = (
                    block[ii * T : (ii + 1) * T, jj * T : (jj + 1) * T] * -scale
                )

    def outer_own():
        for half, jb in ((0, 1), (0, 2), (1, 0), (1, 1)):
            outer(half, jb)

    def outer_halo():
        outer(0, 0)
        outer(1, 2)

    def share(i, k):
        return gsum[i * 6 + i % 2 + offsets[i, k]]

    pair = [
        remote(asend.at[by], arecv.at[by], pair_s.at[by], pair_r.at[by], n, mate)
        for by in range(NX)
    ]

    def send_pair():
        for by in (2, 1, 3, 0):
            for i in range(ROWT):
                asend[by, i] = share(i, at_x(by, 1 - c)).astype(BF16)
            send(None, pair[by])

    def forward():
        def step(q, carry):
            cols = pl.ds(pl.multiple_of(q * COLS, COLS), COLS)
            for half in (0, 1):
                rows = slice(half * HALO, (half + 1) * HALO)
                coupled = dot(
                    band[rows, half * HALO : half * HALO + 3 * HALO],
                    vpad[half * HALO : half * HALO + 3 * HALO, cols],
                    ((1,), (0,)),
                )
                for s in range(COLS // T):
                    part = pl.ds(pl.multiple_of(q * COLS + s * T, T), T)
                    source = drive_b[rows, :] * (state[rows, part].astype(F32) - 1.0)
                    resp[rows, part] = (
                        source - coupled[:, s * T : (s + 1) * T]
                    ) * recip_b[rows, :]
            return carry

        lax.fori_loop(0, CHUNKS, step, 0)

    half = ROWT // 2
    hop = [
        remote(
            hsend.at[side], hrecv.at[side], hop_s.at[side], hop_r.at[side], n, at_x((1, 3)[side], c)
        )
        for side in (0, 1)
    ]
    grad = [
        [
            remote(
                bsend.at[side, pl.ds(part * half, half)],
                brecv.at[side, pl.ds(part * half, half)],
                grad_s.at[side, part],
                grad_r.at[side, part],
                n,
                at_x((1, 3)[side], c),
            )
            for part in (0, 1)
        ]
        for side in (0, 1)
    ]

    def summed(by, i):
        return share(i, at_x(by, c)) + arecv[by, i].astype(F32)

    def send_hop():
        pair[2].wait_recv()
        for side in (0, 1):
            for i in range(half):
                hsend[side, i] = summed(2, side * half + i).astype(BF16)
            send(None, hop[side])

    def send_grad():
        for side in (0, 1):
            by = (1, 3)[side]
            pair[by].wait_recv()
            part = 1 - side
            for i in range(part * half, (part + 1) * half):
                bsend[side, i] = summed(by, i).astype(BF16)
            send(None, grad[side][part])

    def send_rest():
        for side in (0, 1):
            by = (1, 3)[side]
            hop[side].wait_recv()
            for i in range(half):
                bsend[side, side * half + i] = (
                    summed(by, side * half + i) + hrecv[side, i].astype(F32)
                ).astype(BF16)
            send(None, grad[side][side])

    def backward():
        def step(q, carry):
            cols = pl.ds(pl.multiple_of(q * COLS, COLS), COLS)
            for half in (0, 1):
                rows = slice(half * HALO, (half + 1) * HALO)
                back = dot(
                    band[:, HALO + half * HALO : 2 * HALO + half * HALO],
                    lam[:, cols],
                    ((0,), (0,)),
                )
                for s in range(COLS // T):
                    part = pl.ds(pl.multiple_of(q * COLS + s * T, T), T)
                    sgrad[rows, part] = (
                        cot[rows, part].astype(F32) - back[:, s * T : (s + 1) * T]
                    ) * recip_b[rows, :]
            return carry

        lax.fori_loop(0, CHUNKS, step, 0)

    def finish_grad():
        pair[0].wait_recv()
        for i in range(ROWT):
            if i % half == 0:
                for side in (0, 1):
                    grad[side][i // half].wait_recv()
            total = summed(0, i)
            for side in (0, 1):
                total += brecv[side, i].astype(F32)
            tgrad[0, i] = total

    def add(side, q):
        rows = slice(side * HALO, (side + 1) * HALO)
        for s in range(COLS // T):
            part = slice(q * COLS + s * T, q * COLS + (s + 1) * T)
            terms = precv[side, q, :, s * T : (s + 1) * T].astype(F32)
            sgrad[rows, part] -= terms * recip_b[rows, :]

    def finish_back():
        for q in range(EARLY, CHUNKS):

            @pl.when(has_low)
            def _(q=q):
                back_up[q].wait_recv()
                add(0, q)

            @pl.when(has_high)
            def _(q=q):
                back_down[q].wait_recv()
                add(1, q)

    def drain():
        for condition, copy in sent:
            only(condition, copy.wait_send)

    stage_tiles()
    make_volt((0, 1))
    enter()
    send_tiles()
    send_outer()
    make_volt((2, 3))
    send_inner()
    make_lam()
    send_lam()
    clear_band()
    clear_ends()
    outer_own()
    share_tiles()
    relay_tiles()
    wait_tiles()
    fill_first()
    send_corner()
    send_back()
    wait_volt()
    outer_halo()
    send_pair()
    fill_rest()
    forward()
    send_hop()
    send_grad()
    backward()
    send_rest()
    relay_corner()
    finish_grad()
    finish_lam()
    finish_back()
    drain()


def write_out(resp, sgrad, tgrad, resp_hbm, sgrad_hbm, tgrad_hbm, sem):
    copies = [pltpu.make_async_copy(tgrad, tgrad_hbm, sem.at[0])]
    for r in range(ROWT):
        rows = pl.ds(r * T, T)
        copies += [
            pltpu.make_async_copy(resp.at[rows], resp_hbm.at[rows], sem.at[1 + r]),
            pltpu.make_async_copy(sgrad.at[rows], sgrad_hbm.at[rows], sem.at[5 + r]),
        ]
    for copy in copies:
        copy.start()
    for copy in copies:
        copy.wait()


def body(tile_store, send_order, place, offsets, state, drive, conduct, cotangent):
    groups = lax.axis_size("pat")
    scale = 1.0 / float(PATS * groups) ** 0.5
    vmem = pl.BlockSpec(memory_space=pltpu.VMEM)
    hbm = pl.BlockSpec(memory_space=pltpu.HBM)
    dma = pltpu.SemaphoreType.DMA

    def run(*refs):
        kernel(scale, *refs)

    held = pl.pallas_call(
        run,
        out_shape=(
            jax.ShapeDtypeStruct((ROWS, PATS), F32),
            jax.ShapeDtypeStruct((ROWS, PATS), F32),
            jax.ShapeDtypeStruct((1, ROWT, T, T), F32),
        ),
        in_specs=[hbm] * 8,
        out_specs=(vmem, vmem, vmem),
        scratch_shapes=[
            pltpu.VMEM((ROWT, T), F32),
            pltpu.VMEM((ROWT, T), F32),
            pltpu.SMEM((1, NET), jnp.int32),
            pltpu.SMEM((1, NET), jnp.int32),
            pltpu.SMEM((ROWT, K), jnp.int32),
            pltpu.VMEM((NET, T, T), BF16),
            pltpu.VMEM((ROWT, T, T), BF16),
            pltpu.VMEM((NET, T, T), BF16),
            pltpu.VMEM((ROWS, PATS), jnp.int32),
            pltpu.VMEM((ROWS, PATS), BF16),
            pltpu.VMEM((ROWS + 2 * HALO, PATS), BF16),
            pltpu.VMEM((ROWS, PATS), BF16),
            pltpu.VMEM((ROWS, ROWS + 2 * HALO), BF16),
            pltpu.VMEM((ROWS, T), F32),
            pltpu.VMEM((ROWS, T), F32),
            pltpu.VMEM((2, CHUNKS, HALO, COLS), BF16),
            pltpu.VMEM((2, CHUNKS, HALO, COLS), BF16),
            pltpu.VMEM((2, EARLY, HALO, COLS), BF16),
            pltpu.VMEM((2, 2, T, HALO), BF16),
            pltpu.VMEM((24, T, T), F32),
            pltpu.VMEM((NX, ROWT, T, T), BF16),
            pltpu.VMEM((NX, ROWT, T, T), BF16),
            pltpu.VMEM((2, ROWT // 2, T, T), BF16),
            pltpu.VMEM((2, ROWT // 2, T, T), BF16),
            pltpu.VMEM((2, ROWT, T, T), BF16),
            pltpu.VMEM((2, ROWT, T, T), BF16),
            dma((14,)),
            dma((ROWT,)),
            dma((ROWT,)),
            dma((4,)),
            dma((4,)),
            dma((3, ROWT)),
            dma((3, ROWT)),
            dma((4, ROWT)),
            dma((4, ROWT)),
            dma((2, CHUNKS)),
            dma((2, CHUNKS)),
            dma((2, EARLY)),
            dma((2, EARLY)),
            dma((2,)),
            dma((2,)),
            dma((2,)),
            dma((2,)),
            dma((NX,)),
            dma((NX,)),
            dma((2,)),
            dma((2,)),
            dma((2, 2)),
            dma((2, 2)),
        ],
        compiler_params=pltpu.CompilerParams(
            collective_id=0, has_side_effects=True, vmem_limit_bytes=40 * 1024 * 1024
        ),
        name="crosstalk",
    )(
        *[
            pltpu.with_memory_space_constraint(value, pltpu.HBM)
            for value in (
                drive.reshape(ROWT, T),
                conduct.reshape(ROWT, T),
                send_order,
                place,
                offsets,
                tile_store,
                state,
                cotangent,
            )
        ],
    )

    return pl.pallas_call(
        write_out,
        out_shape=[jax.ShapeDtypeStruct(value.shape, value.dtype) for value in held],
        in_specs=[vmem] * 3,
        out_specs=[hbm] * 3,
        scratch_shapes=[dma((9,))],
        compiler_params=pltpu.CompilerParams(vmem_limit_bytes=1024 * 1024),
        name="write_out",
    )(*held)


def solution(mesh):
    placed = (
        P("net", None, None),
        P("net", None),
        P("net", None),
        P("net", None),
        P("net", "pat"),
        P("net"),
        P("net"),
        P("net", "pat"),
    )
    return jax.shard_map(
        body,
        mesh=mesh,
        in_specs=placed,
        out_specs=(P("net", "pat"), P("net", "pat"), P("pat", "net", None, None)),
        check_vma=False,
    )
```

```python
import jax
import jax.numpy as jnp
from jax import lax
from jax.experimental import pallas as pl
from jax.experimental.pallas import tpu as pltpu
from jax.sharding import PartitionSpec as P

MESH = pl.DeviceIdType.MESH
BF16 = jnp.bfloat16
F32 = jnp.float32
T = 128
ROWT = 4
K = 8
ROWS = 512
PATS = 1024
HALO = 256
NET = 32
NZ = 8
NY = 4
NX = 4
COLS = 256
CHUNKS = PATS // COLS


def mod(value, size):
    return lax.rem(value + 4 * size, size)


def dot(a, b, dims):
    return lax.dot_general(a, b, (dims, ((), ())), preferred_element_type=F32)


def kernel(
    scale,
    drive_hbm,
    conduct_hbm,
    order_hbm,
    place_hbm,
    offsets_hbm,
    store_hbm,
    state_hbm,
    cot_hbm,
    resp,
    sgrad,
    tgrad,
    drive,
    conduct,
    order,
    place,
    offsets,
    slots,
    store,
    stage,
    tiles,
    state,
    cot,
    vpad,
    lam,
    band,
    drive_b,
    recip_b,
    psend,
    precv,
    gsum,
    asend,
    arecv,
    hsend,
    hrecv,
    bsend,
    brecv,
    load_sem,
    route_s,
    route_r,
    volt_s,
    volt_r,
    across_s,
    across_r,
    core_s,
    core_r,
    back_s,
    back_r,
    pair_s,
    pair_r,
    hop_s,
    hop_r,
    grad_s,
    grad_r,
):
    n = lax.axis_index("net")
    g = lax.axis_index("pat")
    y, z = n // NZ, lax.rem(n, NZ)
    x, c = g // 2, lax.rem(g, 2)
    mate = g + 1 - 2 * c

    def at_x(by, core):
        return mod(x + by, NX) * 2 + core

    def remote(src, dst, send, recv, net, pat):
        return pltpu.make_async_remote_copy(
            src_ref=src,
            dst_ref=dst,
            send_sem=send,
            recv_sem=recv,
            device_id=(net, pat),
            device_id_type=MESH,
        )

    barrier = pltpu.get_barrier_semaphore()

    def greet(net, pat):
        pl.semaphore_signal(barrier, inc=1, device_id=(net, pat), device_id_type=MESH)

    def source_net(m):
        return mod(y - m, NY) * NZ + mod(z - g - 2 * m, NZ)

    def target_net(m):
        return mod(y + m, NY) * NZ + mod(z + g + 2 * m, NZ)

    for m in (1, 2, 3):
        greet(source_net(m), g)

    @pl.when(g != 0)
    def _():
        greet(source_net(0), g)

    for by in (1, 2, 3):
        greet(n, at_x(by, c))
    greet(n, mate)

    @pl.when(n > 0)
    def _():
        greet(n - 1, g)

    @pl.when(n < NET - 1)
    def _():
        greet(n + 1, g)

    loads = []
    for r in (0, 3, 1, 2):
        rows = pl.ds(r * T, T)
        loads.append(
            pltpu.make_async_copy(state_hbm.at[rows], state.at[rows], load_sem.at[r])
        )
    store_load = pltpu.make_async_copy(store_hbm, store, load_sem.at[8])
    cot_loads = []
    for r in range(ROWT):
        rows = pl.ds(r * T, T)
        cot_loads.append(
            pltpu.make_async_copy(cot_hbm.at[rows], cot.at[rows], load_sem.at[4 + r])
        )
    small = [
        pltpu.make_async_copy(drive_hbm, drive, load_sem.at[9]),
        pltpu.make_async_copy(conduct_hbm, conduct, load_sem.at[10]),
        pltpu.make_async_copy(order_hbm, order, load_sem.at[11]),
        pltpu.make_async_copy(place_hbm, place, load_sem.at[12]),
        pltpu.make_async_copy(offsets_hbm, offsets, load_sem.at[13]),
    ]
    for copy in small + loads[:2] + [store_load] + loads[2:] + cot_loads:
        copy.start()
    for copy in small:
        copy.wait()

    eye = lax.broadcasted_iota(jnp.int32, (T, T), 0) == lax.broadcasted_iota(
        jnp.int32, (T, T), 1
    )
    ratio = []
    for r in range(ROWT):
        d_row = jnp.broadcast_to(drive[r : r + 1, :], (T, T))
        g_row = jnp.broadcast_to(conduct[r : r + 1, :], (T, T))
        d_col = jnp.sum(jnp.where(eye, d_row, 0.0), axis=1, keepdims=True)
        g_col = jnp.sum(jnp.where(eye, g_row, 0.0), axis=1, keepdims=True)
        drive_b[r * T : (r + 1) * T, :] = jnp.broadcast_to(d_col, (T, T))
        recip_b[r * T : (r + 1) * T, :] = jnp.broadcast_to(1.0 / g_col, (T, T))
        ratio.append((d_col / g_col).astype(BF16).astype(F32))

    sent = []

    def only(condition, act):
        if condition is None:
            act()
        else:
            pl.when(condition)(act)

    def send(condition, copy):
        only(condition, copy.start)
        sent.append((condition, copy))

    has_low, has_high = n > 0, n < NET - 1

    def stage_tiles():
        store_load.wait()
        for t in range(ROWT):
            stage[t] = store[order[0, target_net(t)]]

        @pl.when(g == 0)
        def _():
            tiles[0] = store[order[0, n]]

    def make_volt(which):
        for at in which:
            r = (0, 3, 1, 2)[at]
            loads[at].wait()
            rows = slice(r * T, (r + 1) * T)
            levels = state[rows, :].astype(F32) - 1.0
            vpad[HALO + r * T : HALO + (r + 1) * T, :] = (levels * ratio[r]).astype(BF16)

    def clear_ends():
        @pl.when(n == 0)
        def _():
            vpad[0:HALO, :] = jnp.zeros((HALO, PATS), BF16)

        @pl.when(n == NET - 1)
        def _():
            vpad[HALO + ROWS :, :] = jnp.zeros((HALO, PATS), BF16)

    def enter():
        peers = (
            7
            + jnp.where(g != 0, 1, 0)
            + jnp.where(n > 0, 1, 0)
            + jnp.where(n < NET - 1, 1, 0)
        )
        pl.semaphore_wait(barrier, peers)

    def route(t):
        return remote(
            stage.at[t],
            tiles.at[g * ROWT + t],
            route_s.at[t],
            route_r.at[t],
            target_net(t),
            g,
        )

    routes = [route(t) for t in range(ROWT)]
    route_if = [g != 0, None, None, None]

    def send_tiles():
        for t in range(ROWT):
            send(route_if[t], routes[t])

    volt_down, volt_up = [], []
    for h in (0, 1):
        volt_down.append(
            remote(
                vpad.at[pl.ds(HALO + h * T, T)],
                vpad.at[pl.ds(HALO + ROWS + h * T, T)],
                volt_s.at[h],
                volt_r.at[h],
                n - 1,
                g,
            )
        )
        volt_up.append(
            remote(
                vpad.at[pl.ds(ROWS + h * T, T)],
                vpad.at[pl.ds(h * T, T)],
                volt_s.at[2 + h],
                volt_r.at[2 + h],
                n + 1,
                g,
            )
        )

    def send_outer():
        send(has_low, volt_down[0])
        send(has_high, volt_up[1])

    def send_inner():
        send(has_low, volt_down[1])
        send(has_high, volt_up[0])

    def wait_volt():
        for h in (0, 1):
            only(has_low, volt_up[h].wait_recv)
            only(has_high, volt_down[h].wait_recv)

    def make_lam():
        for r in range(ROWT):
            cot_loads[r].wait()
            rows = slice(r * T, (r + 1) * T)
            recip = jnp.broadcast_to(recip_b[rows, :1], (T, PATS))
            lam[rows, :] = (cot[rows, :].astype(F32) * recip).astype(BF16)

    def clear_band():
        for i in range(ROWT):
            for j in range(K):
                if j < i or j > i + 4:
                    band[i * T : (i + 1) * T, j * T : (j + 1) * T] = jnp.zeros((T, T), BF16)

    def slot_of(by, core, t):
        return tiles.at[at_x(by, core) * ROWT + t]

    def across(by, t, source):
        slot = slot_of(source, c, t)
        return remote(
            slot, slot, across_s.at[by - 1, t], across_r.at[by - 1, t], n, at_x(by + source, c)
        )

    def relay(by, t, core):
        slot = slot_of(-by, core, t)
        return remote(slot, slot, core_s.at[by, t], core_r.at[by, t], n, mate)

    def share_tiles():
        for t in range(ROWT):
            only(route_if[t], routes[t].wait_recv)
            for by in (3, 1) if t < 2 else (2, 1, 3):
                send(None, across(by, t, 0))
            send(None, relay(0, t, c))

    def relay_tiles():
        for t in range(ROWT):
            for by in (3, 1):
                across(by, t, -by).wait_recv()
                if t < 2 and by == 3:
                    send(None, across(2, t, -by))
                send(None, relay(by, t, c))
        for t in range(ROWT):
            across(2, t, -2).wait_recv()
            send(None, relay(2, t, c))

    def wait_tiles():
        for by in (0, 1, 3, 2):
            for t in range(ROWT):
                relay(by, t, 1 - c).wait_recv()

    def find_tiles():
        for at in range(ROWT * K):
            owner = place[0, at]
            m = (y - (owner >> 3) + NY) & (NY - 1)
            lane = (z - owner - 2 * m + 2 * NET) & (NZ - 1)
            slots[at] = lane * ROWT + m

    def fill(i, ds):
        totals = [jnp.zeros((T, T), F32) for _ in ds]
        for k in range(K):
            tile = tiles[slots[i * K + k]].astype(F32)
            reach = offsets[i, k]
            totals = [
                total + tile * (reach == d).astype(F32) for total, d in zip(totals, ds)
            ]
        for total, d in zip(totals, ds):
            band[i * T : (i + 1) * T, (i + d) * T : (i + d + 1) * T] = total.astype(BF16)

    def fill_first():
        fill(0, (0, 1))
        fill(1, (0,))
        fill(2, (4,))
        fill(3, (3, 4))

    def fill_rest():
        fill(0, (2, 3, 4))
        fill(1, (1, 2))
        fill(1, (3, 4))
        fill(2, (0, 1))
        fill(2, (2, 3))
        fill(3, (0, 1, 2))

    back_down = [
        remote(psend.at[0, q], precv.at[1, q], back_s.at[0, q], back_r.at[1, q], n - 1, g)
        for q in range(CHUNKS)
    ]
    back_up = [
        remote(psend.at[1, q], precv.at[0, q], back_s.at[1, q], back_r.at[0, q], n + 1, g)
        for q in range(CHUNKS)
    ]

    def send_back():
        low = jnp.transpose(band[0:HALO, 0:HALO])
        high = jnp.transpose(band[HALO:ROWS, 3 * HALO :])
        for q in range(CHUNKS):
            cols = slice(q * COLS, (q + 1) * COLS)
            psend[0, q] = dot(low, lam[0:HALO, cols], ((1,), (0,))).astype(BF16)
            psend[1, q] = dot(high, lam[HALO:ROWS, cols], ((1,), (0,))).astype(BF16)
            send(has_low, back_down[q])
            send(has_high, back_up[q])

    def outer(half, jb):
        start = half * HALO + jb * HALO
        block = dot(
            lam[half * HALO : (half + 1) * HALO, :],
            vpad[start : start + HALO, :],
            ((1,), (1,)),
        )
        for ii in (0, 1):
            for jj in (0, 1):
                gsum[(2 * half + ii) * 6 + 2 * jb + jj] = (
                    block[ii * T : (ii + 1) * T, jj * T : (jj + 1) * T] * -scale
                )

    def outer_own():
        for half, jb in ((0, 1), (0, 2), (1, 0), (1, 1)):
            outer(half, jb)

    def outer_halo():
        outer(0, 0)
        outer(1, 2)

    def share(i, k):
        return gsum[i * 6 + i % 2 + offsets[i, k]]

    pair = [
        remote(asend.at[by], arecv.at[by], pair_s.at[by], pair_r.at[by], n, mate)
        for by in range(NX)
    ]

    def send_pair():
        for by in (2, 1, 3, 0):
            for i in range(ROWT):
                asend[by, i] = share(i, at_x(by, 1 - c)).astype(BF16)
            send(None, pair[by])

    def forward():
        def step(q, carry):
            cols = pl.ds(pl.multiple_of(q * COLS, COLS), COLS)
            for half in (0, 1):
                rows = slice(half * HALO, (half + 1) * HALO)
                coupled = dot(
                    band[rows, half * HALO : half * HALO + 3 * HALO],
                    vpad[half * HALO : half * HALO + 3 * HALO, cols],
                    ((1,), (0,)),
                )
                for s in range(COLS // T):
                    part = pl.ds(pl.multiple_of(q * COLS + s * T, T), T)
                    source = drive_b[rows, :] * (state[rows, part].astype(F32) - 1.0)
                    resp[rows, part] = (
                        source - coupled[:, s * T : (s + 1) * T]
                    ) * recip_b[rows, :]
            return carry

        lax.fori_loop(0, CHUNKS, step, 0)

    half = ROWT // 2
    hop = [
        remote(
            hsend.at[side], hrecv.at[side], hop_s.at[side], hop_r.at[side], n, at_x((1, 3)[side], c)
        )
        for side in (0, 1)
    ]
    grad = [
        [
            remote(
                bsend.at[side, pl.ds(part * half, half)],
                brecv.at[side, pl.ds(part * half, half)],
                grad_s.at[side, part],
                grad_r.at[side, part],
                n,
                at_x((1, 3)[side], c),
            )
            for part in (0, 1)
        ]
        for side in (0, 1)
    ]

    def summed(by, i):
        return share(i, at_x(by, c)) + arecv[by, i].astype(F32)

    def send_hop():
        pair[2].wait_recv()
        for side in (0, 1):
            for i in range(half):
                hsend[side, i] = summed(2, side * half + i).astype(BF16)
            send(None, hop[side])

    def send_grad():
        for side in (0, 1):
            by = (1, 3)[side]
            pair[by].wait_recv()
            part = 1 - side
            for i in range(part * half, (part + 1) * half):
                bsend[side, i] = summed(by, i).astype(BF16)
            send(None, grad[side][part])

    def send_rest():
        for side in (0, 1):
            by = (1, 3)[side]
            hop[side].wait_recv()
            for i in range(half):
                bsend[side, side * half + i] = (
                    summed(by, side * half + i) + hrecv[side, i].astype(F32)
                ).astype(BF16)
            send(None, grad[side][side])

    def backward():
        def step(q, carry):
            cols = pl.ds(pl.multiple_of(q * COLS, COLS), COLS)
            for half in (0, 1):
                rows = slice(half * HALO, (half + 1) * HALO)
                back = dot(
                    band[:, HALO + half * HALO : 2 * HALO + half * HALO],
                    lam[:, cols],
                    ((0,), (0,)),
                )
                for s in range(COLS // T):
                    part = pl.ds(pl.multiple_of(q * COLS + s * T, T), T)
                    sgrad[rows, part] = (
                        cot[rows, part].astype(F32) - back[:, s * T : (s + 1) * T]
                    ) * recip_b[rows, :]
            return carry

        lax.fori_loop(0, CHUNKS, step, 0)

    def finish_grad():
        pair[0].wait_recv()
        for i in range(ROWT):
            if i % half == 0:
                for side in (0, 1):
                    grad[side][i // half].wait_recv()
            total = summed(0, i)
            for side in (0, 1):
                total += brecv[side, i].astype(F32)
            tgrad[0, i] = total

    def add(side, q):
        rows = slice(side * HALO, (side + 1) * HALO)
        for s in range(COLS // T):
            part = slice(q * COLS + s * T, q * COLS + (s + 1) * T)
            terms = precv[side, q, :, s * T : (s + 1) * T].astype(F32)
            sgrad[rows, part] -= terms * recip_b[rows, :]

    def finish_back(chunks):
        for q in chunks:

            @pl.when(has_low)
            def _(q=q):
                back_up[q].wait_recv()
                add(0, q)

            @pl.when(has_high)
            def _(q=q):
                back_down[q].wait_recv()
                add(1, q)

    def drain():
        for condition, copy in sent:
            only(condition, copy.wait_send)

    stage_tiles()
    make_volt((0, 1))
    enter()
    send_tiles()
    send_outer()
    make_volt((2, 3))
    send_inner()
    make_lam()
    clear_band()
    clear_ends()
    find_tiles()
    outer_own()
    share_tiles()
    relay_tiles()
    wait_tiles()
    fill_first()
    send_back()
    wait_volt()
    outer_halo()
    send_pair()
    fill_rest()
    forward()
    send_hop()
    send_grad()
    backward()
    send_rest()
    finish_back(range(CHUNKS - 1))
    finish_grad()
    finish_back(range(CHUNKS - 1, CHUNKS))
    drain()


def write_out(resp, sgrad, tgrad, resp_hbm, sgrad_hbm, tgrad_hbm, sem):
    copies = [pltpu.make_async_copy(tgrad, tgrad_hbm, sem.at[0])]
    for r in range(ROWT):
        rows = pl.ds(r * T, T)
        copies += [
            pltpu.make_async_copy(resp.at[rows], resp_hbm.at[rows], sem.at[1 + r]),
            pltpu.make_async_copy(sgrad.at[rows], sgrad_hbm.at[rows], sem.at[5 + r]),
        ]
    for copy in copies:
        copy.start()
    for copy in copies:
        copy.wait()


def body(tile_store, send_order, place, offsets, state, drive, conduct, cotangent):
    groups = lax.axis_size("pat")
    scale = 1.0 / float(PATS * groups) ** 0.5
    vmem = pl.BlockSpec(memory_space=pltpu.VMEM)
    hbm = pl.BlockSpec(memory_space=pltpu.HBM)
    dma = pltpu.SemaphoreType.DMA

    def run(*refs):
        kernel(scale, *refs)

    held = pl.pallas_call(
        run,
        out_shape=(
            jax.ShapeDtypeStruct((ROWS, PATS), F32),
            jax.ShapeDtypeStruct((ROWS, PATS), F32),
            jax.ShapeDtypeStruct((1, ROWT, T, T), F32),
        ),
        in_specs=[hbm] * 8,
        out_specs=(vmem, vmem, vmem),
        scratch_shapes=[
            pltpu.VMEM((ROWT, T), F32),
            pltpu.VMEM((ROWT, T), F32),
            pltpu.SMEM((1, NET), jnp.int32),
            pltpu.SMEM((1, NET), jnp.int32),
            pltpu.SMEM((ROWT, K), jnp.int32),
            pltpu.SMEM((ROWT * K,), jnp.int32),
            pltpu.VMEM((NET, T, T), BF16),
            pltpu.VMEM((ROWT, T, T), BF16),
            pltpu.VMEM((NET, T, T), BF16),
            pltpu.VMEM((ROWS, PATS), jnp.int32),
            pltpu.VMEM((ROWS, PATS), BF16),
            pltpu.VMEM((ROWS + 2 * HALO, PATS), BF16),
            pltpu.VMEM((ROWS, PATS), BF16),
            pltpu.VMEM((ROWS, ROWS + 2 * HALO), BF16),
            pltpu.VMEM((ROWS, T), F32),
            pltpu.VMEM((ROWS, T), F32),
            pltpu.VMEM((2, CHUNKS, HALO, COLS), BF16),
            pltpu.VMEM((2, CHUNKS, HALO, COLS), BF16),
            pltpu.VMEM((24, T, T), F32),
            pltpu.VMEM((NX, ROWT, T, T), BF16),
            pltpu.VMEM((NX, ROWT, T, T), BF16),
            pltpu.VMEM((2, ROWT // 2, T, T), BF16),
            pltpu.VMEM((2, ROWT // 2, T, T), BF16),
            pltpu.VMEM((2, ROWT, T, T), BF16),
            pltpu.VMEM((2, ROWT, T, T), BF16),
            dma((14,)),
            dma((ROWT,)),
            dma((ROWT,)),
            dma((4,)),
            dma((4,)),
            dma((3, ROWT)),
            dma((3, ROWT)),
            dma((4, ROWT)),
            dma((4, ROWT)),
            dma((2, CHUNKS)),
            dma((2, CHUNKS)),
            dma((NX,)),
            dma((NX,)),
            dma((2,)),
            dma((2,)),
            dma((2, 2)),
            dma((2, 2)),
        ],
        compiler_params=pltpu.CompilerParams(
            collective_id=0, has_side_effects=True, vmem_limit_bytes=40 * 1024 * 1024
        ),
        name="crosstalk",
    )(
        *[
            pltpu.with_memory_space_constraint(value, pltpu.HBM)
            for value in (
                drive.reshape(ROWT, T),
                conduct.reshape(ROWT, T),
                send_order,
                place,
                offsets,
                tile_store,
                state,
                cotangent,
            )
        ],
    )

    return pl.pallas_call(
        write_out,
        out_shape=[jax.ShapeDtypeStruct(value.shape, value.dtype) for value in held],
        in_specs=[vmem] * 3,
        out_specs=[hbm] * 3,
        scratch_shapes=[dma((9,))],
        compiler_params=pltpu.CompilerParams(vmem_limit_bytes=1024 * 1024),
        name="write_out",
    )(*held)


def solution(mesh):
    placed = (
        P("net", None, None),
        P("net", None),
        P("net", None),
        P("net", None),
        P("net", "pat"),
        P("net"),
        P("net"),
        P("net", "pat"),
    )
    return jax.shard_map(
        body,
        mesh=mesh,
        in_specs=placed,
        out_specs=(P("net", "pat"), P("net", "pat"), P("pat", "net", None, None)),
        check_vma=False,
    )
```

```python
import jax
import jax.numpy as jnp
from jax import lax
from jax.experimental import pallas as pl
from jax.experimental.pallas import tpu as pltpu
from jax.sharding import PartitionSpec as P

MESH = pl.DeviceIdType.MESH
BF16 = jnp.bfloat16
F32 = jnp.float32
T = 128
ROWT = 4
K = 8
ROWS = 512
PATS = 1024
HALO = 256
NET = 32
NZ = 8
NY = 4
NX = 4
COLS = 256
CHUNKS = PATS // COLS


def mod(value, size):
    return lax.rem(value + 4 * size, size)


def dot(a, b, dims):
    return lax.dot_general(a, b, (dims, ((), ())), preferred_element_type=F32)


def kernel(
    scale,
    drive_hbm,
    conduct_hbm,
    order_hbm,
    place_hbm,
    offsets_hbm,
    store_hbm,
    state_hbm,
    cot_hbm,
    resp,
    sgrad,
    tgrad,
    drive,
    conduct,
    order,
    place,
    offsets,
    slots,
    store,
    stage,
    tiles,
    state,
    cot,
    vpad,
    lam,
    band,
    drive_b,
    recip_b,
    psend,
    precv,
    gsum,
    asend,
    arecv,
    hsend,
    hrecv,
    bsend,
    brecv,
    load_sem,
    route_s,
    route_r,
    volt_s,
    volt_r,
    across_s,
    across_r,
    core_s,
    core_r,
    back_s,
    back_r,
    pair_s,
    pair_r,
    hop_s,
    hop_r,
    grad_s,
    grad_r,
):
    n = lax.axis_index("net")
    g = lax.axis_index("pat")
    y, z = n // NZ, lax.rem(n, NZ)
    x, c = g // 2, lax.rem(g, 2)
    mate = g + 1 - 2 * c

    def at_x(by, core):
        return mod(x + by, NX) * 2 + core

    def remote(src, dst, send, recv, net, pat):
        return pltpu.make_async_remote_copy(
            src_ref=src,
            dst_ref=dst,
            send_sem=send,
            recv_sem=recv,
            device_id=(net, pat),
            device_id_type=MESH,
        )

    barrier = pltpu.get_barrier_semaphore()

    def greet(net, pat):
        pl.semaphore_signal(barrier, inc=1, device_id=(net, pat), device_id_type=MESH)

    def source_net(m):
        return mod(y - m, NY) * NZ + mod(z - g - 2 * m, NZ)

    def target_net(m):
        return mod(y + m, NY) * NZ + mod(z + g + 2 * m, NZ)

    for m in (1, 2, 3):
        greet(source_net(m), g)

    @pl.when(g != 0)
    def _():
        greet(source_net(0), g)

    for by in (1, 2, 3):
        greet(n, at_x(by, c))
    greet(n, mate)

    @pl.when(n > 0)
    def _():
        greet(n - 1, g)

    @pl.when(n < NET - 1)
    def _():
        greet(n + 1, g)

    loads = []
    for r in (0, 3, 1, 2):
        rows = pl.ds(r * T, T)
        loads.append(
            pltpu.make_async_copy(state_hbm.at[rows], state.at[rows], load_sem.at[r])
        )
    store_load = pltpu.make_async_copy(store_hbm, store, load_sem.at[8])
    cot_loads = []
    for r in range(ROWT):
        rows = pl.ds(r * T, T)
        cot_loads.append(
            pltpu.make_async_copy(cot_hbm.at[rows], cot.at[rows], load_sem.at[4 + r])
        )
    small = [
        pltpu.make_async_copy(drive_hbm, drive, load_sem.at[9]),
        pltpu.make_async_copy(conduct_hbm, conduct, load_sem.at[10]),
        pltpu.make_async_copy(order_hbm, order, load_sem.at[11]),
        pltpu.make_async_copy(place_hbm, place, load_sem.at[12]),
        pltpu.make_async_copy(offsets_hbm, offsets, load_sem.at[13]),
    ]
    for copy in small + loads[:2] + [store_load] + loads[2:] + cot_loads:
        copy.start()
    for copy in small:
        copy.wait()

    eye = lax.broadcasted_iota(jnp.int32, (T, T), 0) == lax.broadcasted_iota(
        jnp.int32, (T, T), 1
    )
    ratio = []
    for r in range(ROWT):
        d_row = jnp.broadcast_to(drive[r : r + 1, :], (T, T))
        g_row = jnp.broadcast_to(conduct[r : r + 1, :], (T, T))
        d_col = jnp.sum(jnp.where(eye, d_row, 0.0), axis=1, keepdims=True)
        g_col = jnp.sum(jnp.where(eye, g_row, 0.0), axis=1, keepdims=True)
        drive_b[r * T : (r + 1) * T, :] = jnp.broadcast_to(d_col, (T, T))
        recip_b[r * T : (r + 1) * T, :] = jnp.broadcast_to(1.0 / g_col, (T, T))
        ratio.append((d_col / g_col).astype(BF16).astype(F32))

    sent = []

    def only(condition, act):
        if condition is None:
            act()
        else:
            pl.when(condition)(act)

    def send(condition, copy):
        only(condition, copy.start)
        sent.append((condition, copy))

    has_low, has_high = n > 0, n < NET - 1

    def stage_tiles():
        store_load.wait()
        for t in range(ROWT):
            stage[t] = store[order[0, target_net(t)]]

        @pl.when(g == 0)
        def _():
            tiles[0] = store[order[0, n]]

    def make_volt(which):
        for at in which:
            r = (0, 3, 1, 2)[at]
            loads[at].wait()
            rows = slice(r * T, (r + 1) * T)
            levels = state[rows, :].astype(F32) - 1.0
            vpad[HALO + r * T : HALO + (r + 1) * T, :] = (levels * ratio[r]).astype(BF16)

    def clear_ends():
        @pl.when(n == 0)
        def _():
            vpad[0:HALO, :] = jnp.zeros((HALO, PATS), BF16)

        @pl.when(n == NET - 1)
        def _():
            vpad[HALO + ROWS :, :] = jnp.zeros((HALO, PATS), BF16)

    def enter():
        peers = (
            7
            + jnp.where(g != 0, 1, 0)
            + jnp.where(n > 0, 1, 0)
            + jnp.where(n < NET - 1, 1, 0)
        )
        pl.semaphore_wait(barrier, peers)

    def route(t):
        return remote(
            stage.at[t],
            tiles.at[g * ROWT + t],
            route_s.at[t],
            route_r.at[t],
            target_net(t),
            g,
        )

    routes = [route(t) for t in range(ROWT)]
    route_if = [g != 0, None, None, None]

    def send_tiles():
        for t in range(ROWT):
            send(route_if[t], routes[t])

    volt_down, volt_up = [], []
    for h in (0, 1):
        volt_down.append(
            remote(
                vpad.at[pl.ds(HALO + h * T, T)],
                vpad.at[pl.ds(HALO + ROWS + h * T, T)],
                volt_s.at[h],
                volt_r.at[h],
                n - 1,
                g,
            )
        )
        volt_up.append(
            remote(
                vpad.at[pl.ds(ROWS + h * T, T)],
                vpad.at[pl.ds(h * T, T)],
                volt_s.at[2 + h],
                volt_r.at[2 + h],
                n + 1,
                g,
            )
        )

    def send_outer():
        send(has_low, volt_down[0])
        send(has_high, volt_up[1])

    def send_inner():
        send(has_low, volt_down[1])
        send(has_high, volt_up[0])

    def wait_volt():
        for h in (0, 1):
            only(has_low, volt_up[h].wait_recv)
            only(has_high, volt_down[h].wait_recv)

    def make_lam():
        for r in range(ROWT):
            cot_loads[r].wait()
            rows = slice(r * T, (r + 1) * T)
            recip = jnp.broadcast_to(recip_b[rows, :1], (T, PATS))
            lam[rows, :] = (cot[rows, :].astype(F32) * recip).astype(BF16)

    def clear_band():
        for i in range(ROWT):
            for j in range(K):
                if j < i or j > i + 4:
                    band[i * T : (i + 1) * T, j * T : (j + 1) * T] = jnp.zeros((T, T), BF16)

    def slot_of(by, core, t):
        return tiles.at[at_x(by, core) * ROWT + t]

    def across(by, t, source):
        slot = slot_of(source, c, t)
        return remote(
            slot, slot, across_s.at[by - 1, t], across_r.at[by - 1, t], n, at_x(by + source, c)
        )

    def relay(by, t, core):
        slot = slot_of(-by, core, t)
        return remote(slot, slot, core_s.at[by, t], core_r.at[by, t], n, mate)

    def share_tiles():
        for t in range(ROWT):
            only(route_if[t], routes[t].wait_recv)
            for by in (3, 1) if t < 2 else (2, 1, 3):
                send(None, across(by, t, 0))
            send(None, relay(0, t, c))

    def relay_tiles():
        for t in range(ROWT):
            for by in (3, 1):
                across(by, t, -by).wait_recv()
                if t < 2 and by == 3:
                    send(None, across(2, t, -by))
                send(None, relay(by, t, c))
        for t in range(ROWT):
            across(2, t, -2).wait_recv()
            send(None, relay(2, t, c))

    def wait_tiles():
        for by in (0, 1, 3, 2):
            for t in range(ROWT):
                relay(by, t, 1 - c).wait_recv()

    def find_tiles():
        for at in range(ROWT * K):
            owner = place[0, at]
            m = (y - (owner >> 3) + NY) & (NY - 1)
            lane = (z - owner - 2 * m + 2 * NET) & (NZ - 1)
            slots[at] = lane * ROWT + m

    def fill(i, ds):
        totals = [jnp.zeros((T, T), F32) for _ in ds]
        for k in range(K):
            tile = tiles[slots[i * K + k]].astype(F32)
            reach = offsets[i, k]
            totals = [
                total + tile * (reach == d).astype(F32) for total, d in zip(totals, ds)
            ]
        for total, d in zip(totals, ds):
            band[i * T : (i + 1) * T, (i + d) * T : (i + d + 1) * T] = total.astype(BF16)

    def fill_first():
        fill(0, (0, 1))
        fill(1, (0,))
        fill(2, (4,))
        fill(3, (3, 4))

    def fill_rest():
        fill(0, (2, 3, 4))
        fill(1, (1, 2))
        fill(1, (3, 4))
        fill(2, (0, 1))
        fill(2, (2, 3))
        fill(3, (0, 1, 2))

    back_down = [
        remote(psend.at[0, q], precv.at[1, q], back_s.at[0, q], back_r.at[1, q], n - 1, g)
        for q in range(CHUNKS)
    ]
    back_up = [
        remote(psend.at[1, q], precv.at[0, q], back_s.at[1, q], back_r.at[0, q], n + 1, g)
        for q in range(CHUNKS)
    ]

    def send_back():
        low = jnp.transpose(band[0:HALO, 0:HALO])
        high = jnp.transpose(band[HALO:ROWS, 3 * HALO :])
        for q in range(CHUNKS):
            cols = slice(q * COLS, (q + 1) * COLS)
            psend[0, q] = dot(low, lam[0:HALO, cols], ((1,), (0,))).astype(BF16)
            psend[1, q] = dot(high, lam[HALO:ROWS, cols], ((1,), (0,))).astype(BF16)
            send(has_low, back_down[q])
            send(has_high, back_up[q])

    def outer(half, jb):
        start = half * HALO + jb * HALO
        block = dot(
            lam[half * HALO : (half + 1) * HALO, :],
            vpad[start : start + HALO, :],
            ((1,), (1,)),
        )
        for ii in (0, 1):
            for jj in (0, 1):
                gsum[(2 * half + ii) * 6 + 2 * jb + jj] = (
                    block[ii * T : (ii + 1) * T, jj * T : (jj + 1) * T] * -scale
                )

    def outer_own():
        for half, jb in ((0, 1), (0, 2), (1, 0), (1, 1)):
            outer(half, jb)

    def outer_halo():
        outer(0, 0)
        outer(1, 2)

    def share(i, k):
        return gsum[i * 6 + i % 2 + offsets[i, k]]

    pair = [
        remote(asend.at[by], arecv.at[by], pair_s.at[by], pair_r.at[by], n, mate)
        for by in range(NX)
    ]

    def send_pair():
        for by in (2, 1, 3, 0):
            for i in range(ROWT):
                asend[by, i] = share(i, at_x(by, 1 - c)).astype(BF16)
            send(None, pair[by])

    def forward():
        def step(q, carry):
            cols = pl.ds(pl.multiple_of(q * COLS, COLS), COLS)
            for half in (0, 1):
                rows = slice(half * HALO, (half + 1) * HALO)
                coupled = dot(
                    band[rows, half * HALO : half * HALO + 3 * HALO],
                    vpad[half * HALO : half * HALO + 3 * HALO, cols],
                    ((1,), (0,)),
                )
                for s in range(COLS // T):
                    part = pl.ds(pl.multiple_of(q * COLS + s * T, T), T)
                    source = drive_b[rows, :] * (state[rows, part].astype(F32) - 1.0)
                    resp[rows, part] = (
                        source - coupled[:, s * T : (s + 1) * T]
                    ) * recip_b[rows, :]
            return carry

        lax.fori_loop(0, CHUNKS, step, 0)

    half = ROWT // 2
    hop = [
        remote(
            hsend.at[side], hrecv.at[side], hop_s.at[side], hop_r.at[side], n, at_x((1, 3)[side], c)
        )
        for side in (0, 1)
    ]
    grad = [
        [
            remote(
                bsend.at[side, pl.ds(part * half, half)],
                brecv.at[side, pl.ds(part * half, half)],
                grad_s.at[side, part],
                grad_r.at[side, part],
                n,
                at_x((1, 3)[side], c),
            )
            for part in (0, 1)
        ]
        for side in (0, 1)
    ]

    def summed(by, i):
        return share(i, at_x(by, c)) + arecv[by, i].astype(F32)

    def send_hop():
        pair[2].wait_recv()
        for side in (0, 1):
            for i in range(half):
                hsend[side, i] = summed(2, side * half + i).astype(BF16)
            send(None, hop[side])

    def send_grad():
        for side in (0, 1):
            by = (1, 3)[side]
            pair[by].wait_recv()
            part = 1 - side
            for i in range(part * half, (part + 1) * half):
                bsend[side, i] = summed(by, i).astype(BF16)
            send(None, grad[side][part])

    def send_rest():
        for side in (0, 1):
            by = (1, 3)[side]
            hop[side].wait_recv()
            for i in range(half):
                bsend[side, side * half + i] = (
                    summed(by, side * half + i) + hrecv[side, i].astype(F32)
                ).astype(BF16)
            send(None, grad[side][side])

    def backward():
        def step(q, carry):
            cols = pl.ds(pl.multiple_of(q * COLS, COLS), COLS)
            for half in (0, 1):
                rows = slice(half * HALO, (half + 1) * HALO)
                back = dot(
                    band[:, HALO + half * HALO : 2 * HALO + half * HALO],
                    lam[:, cols],
                    ((0,), (0,)),
                )
                for s in range(COLS // T):
                    part = pl.ds(pl.multiple_of(q * COLS + s * T, T), T)
                    sgrad[rows, part] = (
                        cot[rows, part].astype(F32) - back[:, s * T : (s + 1) * T]
                    ) * recip_b[rows, :]
            return carry

        lax.fori_loop(0, CHUNKS, step, 0)

    def finish_grad():
        pair[0].wait_recv()
        for i in range(ROWT):
            if i % half == 0:
                for side in (0, 1):
                    grad[side][i // half].wait_recv()
            total = summed(0, i)
            for side in (0, 1):
                total += brecv[side, i].astype(F32)
            tgrad[0, i] = total

    def add(side, q):
        rows = slice(side * HALO, (side + 1) * HALO)
        for s in range(COLS // T):
            part = slice(q * COLS + s * T, q * COLS + (s + 1) * T)
            terms = precv[side, q, :, s * T : (s + 1) * T].astype(F32)
            sgrad[rows, part] -= terms * recip_b[rows, :]

    def finish_back(chunks):
        for q in chunks:

            @pl.when(has_low)
            def _(q=q):
                back_up[q].wait_recv()
                add(0, q)

            @pl.when(has_high)
            def _(q=q):
                back_down[q].wait_recv()
                add(1, q)

    def drain():
        for condition, copy in sent:
            only(condition, copy.wait_send)

    stage_tiles()
    make_volt((0, 1))
    enter()
    send_tiles()
    send_outer()
    make_volt((2, 3))
    send_inner()
    make_lam()
    clear_band()
    clear_ends()
    find_tiles()
    outer_own()
    share_tiles()
    relay_tiles()
    wait_tiles()
    fill_first()
    send_back()
    wait_volt()
    outer_halo()
    send_pair()
    fill_rest()
    forward()
    send_hop()
    send_grad()
    backward()
    send_rest()
    finish_back(range(CHUNKS - 1))
    finish_grad()
    drain()
    finish_back(range(CHUNKS - 1, CHUNKS))


def write_out(resp, sgrad, tgrad, resp_hbm, sgrad_hbm, tgrad_hbm, sem):
    copies = [pltpu.make_async_copy(tgrad, tgrad_hbm, sem.at[0])]
    for r in range(ROWT):
        rows = pl.ds(r * T, T)
        copies += [
            pltpu.make_async_copy(resp.at[rows], resp_hbm.at[rows], sem.at[1 + r]),
            pltpu.make_async_copy(sgrad.at[rows], sgrad_hbm.at[rows], sem.at[5 + r]),
        ]
    for copy in copies:
        copy.start()
    for copy in copies:
        copy.wait()


def body(tile_store, send_order, place, offsets, state, drive, conduct, cotangent):
    groups = lax.axis_size("pat")
    scale = 1.0 / float(PATS * groups) ** 0.5
    vmem = pl.BlockSpec(memory_space=pltpu.VMEM)
    hbm = pl.BlockSpec(memory_space=pltpu.HBM)
    dma = pltpu.SemaphoreType.DMA

    def run(*refs):
        kernel(scale, *refs)

    held = pl.pallas_call(
        run,
        out_shape=(
            jax.ShapeDtypeStruct((ROWS, PATS), F32),
            jax.ShapeDtypeStruct((ROWS, PATS), F32),
            jax.ShapeDtypeStruct((1, ROWT, T, T), F32),
        ),
        in_specs=[hbm] * 8,
        out_specs=(vmem, vmem, vmem),
        scratch_shapes=[
            pltpu.VMEM((ROWT, T), F32),
            pltpu.VMEM((ROWT, T), F32),
            pltpu.SMEM((1, NET), jnp.int32),
            pltpu.SMEM((1, NET), jnp.int32),
            pltpu.SMEM((ROWT, K), jnp.int32),
            pltpu.SMEM((ROWT * K,), jnp.int32),
            pltpu.VMEM((NET, T, T), BF16),
            pltpu.VMEM((ROWT, T, T), BF16),
            pltpu.VMEM((NET, T, T), BF16),
            pltpu.VMEM((ROWS, PATS), jnp.int32),
            pltpu.VMEM((ROWS, PATS), BF16),
            pltpu.VMEM((ROWS + 2 * HALO, PATS), BF16),
            pltpu.VMEM((ROWS, PATS), BF16),
            pltpu.VMEM((ROWS, ROWS + 2 * HALO), BF16),
            pltpu.VMEM((ROWS, T), F32),
            pltpu.VMEM((ROWS, T), F32),
            pltpu.VMEM((2, CHUNKS, HALO, COLS), BF16),
            pltpu.VMEM((2, CHUNKS, HALO, COLS), BF16),
            pltpu.VMEM((24, T, T), F32),
            pltpu.VMEM((NX, ROWT, T, T), BF16),
            pltpu.VMEM((NX, ROWT, T, T), BF16),
            pltpu.VMEM((2, ROWT // 2, T, T), BF16),
            pltpu.VMEM((2, ROWT // 2, T, T), BF16),
            pltpu.VMEM((2, ROWT, T, T), BF16),
            pltpu.VMEM((2, ROWT, T, T), BF16),
            dma((14,)),
            dma((ROWT,)),
            dma((ROWT,)),
            dma((4,)),
            dma((4,)),
            dma((3, ROWT)),
            dma((3, ROWT)),
            dma((4, ROWT)),
            dma((4, ROWT)),
            dma((2, CHUNKS)),
            dma((2, CHUNKS)),
            dma((NX,)),
            dma((NX,)),
            dma((2,)),
            dma((2,)),
            dma((2, 2)),
            dma((2, 2)),
        ],
        compiler_params=pltpu.CompilerParams(
            collective_id=0, has_side_effects=True, vmem_limit_bytes=40 * 1024 * 1024
        ),
        name="crosstalk",
    )(
        *[
            pltpu.with_memory_space_constraint(value, pltpu.HBM)
            for value in (
                drive.reshape(ROWT, T),
                conduct.reshape(ROWT, T),
                send_order,
                place,
                offsets,
                tile_store,
                state,
                cotangent,
            )
        ],
    )

    return pl.pallas_call(
        write_out,
        out_shape=[jax.ShapeDtypeStruct(value.shape, value.dtype) for value in held],
        in_specs=[vmem] * 3,
        out_specs=[hbm] * 3,
        scratch_shapes=[dma((9,))],
        compiler_params=pltpu.CompilerParams(vmem_limit_bytes=1024 * 1024),
        name="write_out",
    )(*held)


def solution(mesh):
    placed = (
        P("net", None, None),
        P("net", None),
        P("net", None),
        P("net", None),
        P("net", "pat"),
        P("net"),
        P("net"),
        P("net", "pat"),
    )
    return jax.shard_map(
        body,
        mesh=mesh,
        in_specs=placed,
        out_specs=(P("net", "pat"), P("net", "pat"), P("pat", "net", None, None)),
        check_vma=False,
    )
```
